32 devices in a mesh: dev: 32 (over z, y, x, core).
Axes of the slice: x: 2, y: 2, z: 4, core: 2. Of those that a mesh axis runs over, the one named last changes fastest.
Arguments:
- features: bfloat16 [16384, 1024], P('dev'), may hold values from -6 to 6
- w_hidden: bfloat16 [1024, 512], replicated, may hold values from -0.1875 to 0.1875
- w_out: bfloat16 [512, 128], replicated, may hold values from -0.25 to 0.25
- items: bfloat16 [65536, 128], P('dev'), may hold values from -200 to 200
- routes: int32 [16384, 4], P('dev'), may hold values from 0 to 511, all different within a row; in each aligned block of 512 rows (0 to 511, 512 to 1023, ...) at most 8 rows name the same one
- cluster_slot: int32 [512], replicated, may hold values from 0 to 511, each once
- sample_ids: int32 [512, 4096], P('dev'), may hold values from 0 to 127
- sample_counts: int32 [512, 4096], P('dev'), may hold values from 1 to 4095
- positives: int32 [16384, 4], P('dev'), may hold values from 0 to 4095
Outputs:
- slot_loss: float32 [512], P('dev')
- grad_hidden: float32 [1024, 512], replicated
- grad_out: float32 [512, 128], replicated
- item_grad: float32 [65536, 128], P('dev')
The draws below stay inside these ranges and needn't reach their ends.
Inputs may be any that keep to these rules, and one draw needn't show every extreme that they name: `routes`: each row names 4 different clusters; within the rows of one device no cluster is named more than 8 times; every cluster is named by some row. `cluster_slot`: each cluster has one slot.
All inputs are finite; a program needn't handle non-finite values.
Results may differ from the reference program's by a relative error of at most 0.012.
The reference program's roundings to bfloat16 on the way (of `hidden`, `query`, `weight`, `dquery`, `dq_total` and `dpre`) count: a program that leaves them out, or rounds other values in their place, can miss the bound.
Values may be sent and summed in bfloat16 or wider, within the bound.
A program may use at most 128 MiB of HBM per device.

```python
import math
import jax
import jax.numpy as jnp
import numpy as np
from jax import lax

FEAT = 1024
HID = 512
EMB = 128
ROUTES = 4
U_DEV = 512
CL_DEV = 16
SAMPLES = 4096
ITEM_CL = 128
ITEM_DEV = 2048
USERS = 16384
CLUSTERS = 512
CAP = 8
ITEMS = 65536
N_DEV = 32


def draw_items(key, part):
    keys = jax.random.split(jax.random.fold_in(key, 17), 1)
    base = jax.random.normal(keys[0], (ITEMS, EMB), jnp.float32) * EMB ** (-0.5)
    return base.astype(jnp.bfloat16)


def place_ends(drawn, own_key, smallest, high):
    longest = drawn.shape.index(max(drawn.shape))
    spots = []
    for shift in (0, 1):
        where = [jax.random.randint(jax.random.fold_in(own_key, axis), (), 0, length) for axis, length in enumerate(drawn.shape)]
        where[longest] = (where[longest] + shift) % drawn.shape[longest]
        spots.append(tuple(where))
    return drawn.at[spots[0]].set(smallest).at[spots[1]].set(high)


def block_levels(own_key, shape, cuts, smallest, top_value):
    def one(axis_at, parts):
        heights = jax.random.uniform(jax.random.fold_in(jax.random.fold_in(own_key, 6), axis_at), (parts,), jnp.float32, smallest / len(cuts), top_value / len(cuts))
        return jnp.repeat(jnp.exp(heights), shape[axis_at] // parts).reshape((-1,) + (1,) * (len(shape) - axis_at - 1))

    gain = one(*cuts[0])
    for cut in cuts[1:]:
        gain = gain * one(*cut)
    return gain


def assign_block(key, own, number, rows, amount, top, bound, lean):
    order = jax.random.permutation(key, amount)
    packed, usual = portions_of(amount, rows * top, bound, lean, True), portions_of(amount, rows * top, bound, lean, False)
    places = jnp.arange(amount)

    def named(sizes, rotation):
        used = int((sizes > 0).sum())
        fixed = max(1, used // 4)
        shifted = fixed + (places - fixed + rotation * (used - fixed)) % max(1, amount - fixed)
        return jnp.zeros((amount,), jnp.int32).at[order[jnp.where(places < fixed, places, shifted)]].set(jnp.asarray(sizes, jnp.int32))

    sizes = jnp.where(number % 4 == 0, named(packed, number // 4), named(usual, number - number // 4 - 1))
    mixed = jax.random.permutation(jax.random.fold_in(own, 3), amount)
    giver, taker = mixed[0:amount // 2 * 2:2], mixed[1:amount // 2 * 2:2]
    slack = jnp.minimum(sizes[giver] - 1, bound - sizes[taker]) // 2
    slack = jnp.where((giver == order[0]) | (taker == order[0]) | (sizes[taker] == 0), 0, jnp.maximum(slack, 0))
    shifted = jax.random.randint(jax.random.fold_in(own, 4), (amount // 2,), 0, 1 << 20) % (slack + 1)
    sizes = sizes.at[giver].add(-shifted).at[taker].add(shifted)
    labels = jnp.searchsorted(jnp.cumsum(sizes), jnp.arange(rows * top), side="right").astype(jnp.int32)
    grid = labels.reshape(top, rows).T
    grid = grid[jax.random.permutation(jax.random.fold_in(own, 1), rows)]
    rotation = jax.random.randint(jax.random.fold_in(own, 2), (rows, 1), 0, top)
    return jnp.take_along_axis(grid, (jnp.arange(top)[None, :] + rotation) % top, axis=1)


def portions_of(amount, total, bound, slope, full):
    loads = [(1 << 20) // math.isqrt(standing ** slope) + 1 for standing in range(1, amount + 1)]
    largest = bound if full else min(bound, max(-(-total // amount), total * loads[0] // sum(loads)))
    least = 1 if total - largest >= amount - 1 else 0
    holding, spare = [largest] + [least] * (amount - 1), total - largest - least * (amount - 1)
    while spare > 0:
        free = [i for i in range(1, amount) if holding[i] < largest] or [i for i in range(1, amount) if holding[i] < bound]
        whole, left = sum([loads[i] for i in free]), spare
        for i in free:
            more = min(bound - holding[i], max(1, left * loads[i] // whole), spare)
            holding[i] = holding[i] + more
            spare = spare - more
    return np.array(holding)


def gaussian(stream_key, extent, spread, limit, shards=(), kind=jnp.bfloat16):
    array = jax.random.normal(stream_key, extent, jnp.float32) * spread
    if len(shards) > 0:
        array = block_levels(stream_key, extent, shards, -0.22, 0.18) * array
    return jnp.clip(array, min=-limit, max=limit).astype(kind)


def setup_inputs(seed: int = 0) -> dict:
    arg_keys = jax.random.split(jax.random.key(seed), 10)
    features = gaussian(arg_keys[0], (USERS, FEAT), 1.0, 6.0, ((0, 32),))
    w_hidden = gaussian(arg_keys[1], (FEAT, HID), FEAT ** -0.5, 0.1875)
    w_out = gaussian(arg_keys[2], (HID, EMB), HID ** -0.5, 0.25)
    items = draw_items(jax.random.fold_in(arg_keys[9], 71), 0)
    routes_keys = jax.random.split(jax.random.fold_in(arg_keys[4], 1), USERS // U_DEV)
    routes_turns = jax.random.permutation(jax.random.fold_in(arg_keys[4], 3), USERS // U_DEV)
    routes = jax.vmap(lambda own, number: assign_block(jax.random.fold_in(arg_keys[4], 2), own, number, U_DEV, CLUSTERS, ROUTES, CAP, 2))(routes_keys, routes_turns).reshape((USERS, ROUTES))
    cluster_slot = jax.random.permutation(arg_keys[5], CLUSTERS).astype(jnp.int32)
    sample_ids = place_ends(jax.random.randint(arg_keys[6], (CLUSTERS, SAMPLES), 0, ITEM_CL), jax.random.fold_in(arg_keys[6], 1), 0, ITEM_CL - 1).astype(jnp.int32)
    sample_counts = place_ends(jax.random.randint(arg_keys[7], (CLUSTERS, SAMPLES), 1, 4096), jax.random.fold_in(arg_keys[7], 1), 1, 4095).astype(jnp.int32)
    positives = place_ends(jax.random.randint(arg_keys[8], (USERS, ROUTES), 0, SAMPLES), jax.random.fold_in(arg_keys[8], 1), 0, SAMPLES - 1).astype(jnp.int32)
    return dict(features=features, w_hidden=w_hidden, w_out=w_out, items=items, routes=routes, cluster_slot=cluster_slot, sample_ids=sample_ids, sample_counts=sample_counts, positives=positives)


def silu_grad(value):
    sig = jax.nn.sigmoid(value)
    return sig * (1.0 + value * (1.0 - sig))

def slot_ranks(keys):
    order = jnp.argsort(keys, stable=True).astype(jnp.int32)
    sorted_keys = keys[order]
    first = jnp.searchsorted(sorted_keys, sorted_keys, side='left').astype(jnp.int32)
    ranked = jnp.arange(keys.shape[0], dtype=jnp.int32) - first
    return jnp.zeros_like(keys).at[order].set(ranked)

def score_block(queries, targets, table, counts):
    scores = jnp.einsum('cqe,cse->cqs', queries.astype(jnp.float32), table.astype(jnp.float32))
    scores = scores - jnp.log(counts.astype(jnp.float32))[:, None, :]
    top = lax.optimization_barrier(jnp.max(scores, axis=2, keepdims=True))
    expo = jnp.exp(scores - top)
    total = lax.optimization_barrier(jnp.sum(expo, axis=2, keepdims=True))
    hit = lax.broadcasted_iota(jnp.int32, scores.shape, 2) == targets[:, :, None]
    picked = lax.optimization_barrier(jnp.sum(jnp.where(hit, scores, 0.0), axis=2))
    losses = jnp.log(total[:, :, 0]) + top[:, :, 0] - picked
    live = targets >= 0
    cluster_loss = lax.optimization_barrier(jnp.sum(jnp.where(live, losses, 0.0), axis=1)) / lax.optimization_barrier(jnp.sum(live.astype(jnp.float32), axis=1))
    weight = (expo / total - hit.astype(jnp.float32)).astype(jnp.bfloat16)
    dquery = jnp.einsum('cqs,cse->cqe', weight.astype(jnp.float32), table.astype(jnp.float32)).astype(jnp.bfloat16)
    dtable = jnp.einsum('cqs,cqe->cse', weight.astype(jnp.float32), queries.astype(jnp.float32))
    return (cluster_loss, dquery, dtable)

def pick_rows(block, ids):
    return block[ids]

def sum_rows(values, ids):
    return jax.ops.segment_sum(values, ids, num_segments=ITEM_CL)

def reference(features, w_hidden, w_out, items, routes, cluster_slot, sample_ids, sample_counts, positives):
    pre = jnp.dot(features, w_hidden, preferred_element_type=jnp.float32)
    hidden = jax.nn.silu(pre).astype(jnp.bfloat16)
    query = jnp.dot(hidden, w_out, preferred_element_type=jnp.float32).astype(jnp.bfloat16)
    users = features.shape[0]
    slots = cluster_slot[routes]
    source = jnp.broadcast_to((jnp.arange(users, dtype=jnp.int32) // U_DEV)[:, None], slots.shape)
    keys = (source * CLUSTERS + slots).reshape(-1)
    ranks = slot_ranks(keys)
    column = source.reshape(-1) * CAP + ranks
    row = slots.reshape(-1)
    width = N_DEV * CAP
    qbuf = jnp.zeros((CLUSTERS, width, EMB), jnp.bfloat16).at[row, column].set(jnp.repeat(query, ROUTES, axis=0))
    tbuf = jnp.full((CLUSTERS, width), -1, jnp.int32).at[row, column].set(positives.reshape(-1))

    def owner(carry, index):
        start = (index * CL_DEV).astype(jnp.int32)
        queries = lax.dynamic_slice_in_dim(qbuf, start, CL_DEV, 0)
        targets = lax.dynamic_slice_in_dim(tbuf, start, CL_DEV, 0)
        table_ids = lax.dynamic_slice_in_dim(sample_ids, start, CL_DEV, 0)
        counts = lax.dynamic_slice_in_dim(sample_counts, start, CL_DEV, 0)
        block_rows = lax.dynamic_slice_in_dim(items, (index * ITEM_DEV).astype(jnp.int32), ITEM_DEV, 0)
        block_rows = block_rows.reshape(CL_DEV, ITEM_CL, EMB)
        table = jax.vmap(pick_rows)(block_rows, table_ids)
        cluster_loss, dquery, dtable = score_block(queries, targets, table, counts)
        grads = jax.vmap(sum_rows)(dtable, table_ids)
        return (carry, (cluster_loss, dquery, grads))
    _, (losses, dqbuf, igrad) = lax.scan(owner, jnp.zeros((), jnp.float32), jnp.arange(N_DEV, dtype=jnp.int32))
    slot_loss = losses.reshape(-1)
    item_grad = igrad.reshape(ITEMS, EMB)
    dq_pairs = dqbuf.reshape(CLUSTERS, width, EMB)[row, column].astype(jnp.float32).reshape(users, ROUTES, EMB)
    dq_total = lax.optimization_barrier(jnp.sum(dq_pairs, axis=1)).astype(jnp.bfloat16)
    grad_out = jnp.dot(hidden.T, dq_total, preferred_element_type=jnp.float32)
    dhidden = jnp.dot(dq_total, w_out.T, preferred_element_type=jnp.float32)
    dpre = (dhidden * silu_grad(pre)).astype(jnp.bfloat16)
    grad_hidden = jnp.dot(features.T, dpre, preferred_element_type=jnp.float32)
    return (slot_loss, grad_hidden, grad_out, item_grad)
```

```python
import functools

import jax
import jax.numpy as jnp
from jax import lax
from jax.experimental import pallas as pl
from jax.experimental.pallas import tpu as pltpu
from jax.sharding import PartitionSpec as P

LINE = 4
LANES = 128
TILE = 8
MESH = pl.DeviceIdType.MESH
F32, BF16, I32 = jnp.float32, jnp.bfloat16, jnp.int32
VMEM_BYTES = 67_000_000


def iota(shape, axis):
    return lax.broadcasted_iota(I32, shape, axis)


def flags(test):
    return jnp.where(test, 1.0, 0.0).astype(BF16)


def log2(value):
    return value.bit_length() - 1


def flip(index, other, size):
    result = index
    weight = 1
    while weight < size:
        mine = (index // weight) % 2
        theirs = (other // weight) % 2
        result = result + weight * (theirs - 2 * mine * theirs)
        weight *= 2
    return result


def each(low, high, action):
    def body(i, carry):
        action(i)
        return carry

    lax.fori_loop(low, high, body, 0)


def remote(src, dst, sems, at, device):
    return pltpu.make_async_remote_copy(
        src_ref=src,
        dst_ref=dst,
        send_sem=sems.at[(0,) + at],
        recv_sem=sems.at[(1,) + at],
        device_id=(device,),
        device_id_type=MESH,
    )


def split(devices, elements):
    unit = devices * TILE
    units = -(-(elements // LANES) // unit)
    first = min(units - 1, max(1, (units * 7 + 4) // 9)) if units > 1 else 1
    return units, first


def step_kernel(
    line,
    plane,
    cap,
    features_hbm,
    w_hidden_hbm,
    w_out_hbm,
    items_hbm,
    ids_hbm,
    counts_hbm,
    routes_hbm,
    spots_hbm,
    slot_hbm,
    loss_out,
    big_out,
    small_out,
    table_out,
    features,
    features_t,
    w_hidden,
    w_out,
    items,
    ids,
    counts,
    routes_ref,
    spots_ref,
    slot_ref,
    slope,
    hidden,
    metas,
    qline,
    earlier,
    codes,
    sel,
    stage,
    got,
    zstage,
    zgot,
    lookup,
    mass,
    tpos,
    wts,
    dqs,
    ret,
    pstage,
    part,
    acc,
    outb,
    core_in,
    a1_in,
    a2_in,
    b1_in,
    b2_in,
    full,
    load_sem,
    m_sem,
    q_sem,
    x_sem,
    t_sem,
    r_sem,
    p_sem,
    c_sem,
    a1_sem,
    a2_sem,
    b1_sem,
    b2_sem,
    az_sem,
    ac_sem,
    ao_sem,
    bz_sem,
    bc_sem,
    bo_sem,
):
    me = lax.axis_index("dev")
    z, p = me // plane, me % plane

    def along(j):
        return flip(z, j, line) * plane + p

    def inside(i):
        return z * plane + flip(p, i, plane)

    visits, users = routes_ref.shape
    clusters = slot_ref.shape[1]
    local_clusters, samples = ids.shape
    item_rows, width = items.shape[1:]
    rows = local_clusters * cap
    hosted = plane * local_clusters
    seats = line * plane * cap
    groups = samples // LANES

    loads = [
        pltpu.make_async_copy(src, dst, load_sem.at[n])
        for n, (src, dst) in enumerate(
            [
                (slot_hbm, slot_ref),
                (routes_hbm, routes_ref),
                (spots_hbm, spots_ref),
                (features_hbm, features),
                (w_hidden_hbm, w_hidden),
                (w_out_hbm, w_out),
                (ids_hbm, ids),
                (counts_hbm, counts),
                (items_hbm, items),
            ]
        )
    ]
    for load in loads:
        load.start()

    barrier = pltpu.get_barrier_semaphore()
    for j in range(1, line):
        pl.semaphore_signal(barrier, inc=1, device_id=(along(j),), device_id_type=MESH)
    each(
        1,
        plane,
        lambda i: pl.semaphore_signal(
            barrier, inc=1, device_id=(inside(i),), device_id_type=MESH
        ),
    )

    earlier[...] = flags(iota((users, users), 0) < iota((users, users), 1))
    for load in loads[:3]:
        load.wait()
    k = iota((hosted, 1), 0)
    host = lax.bitwise_xor(lax.shift_right_logical(k, log2(local_clusters)), p)
    slot = (z * plane + host) * local_clusters + (k & (local_clusters - 1))
    names = jnp.sum(
        jnp.where(slot_ref[...] == slot, iota((hosted, clusters), 1), 0).astype(F32),
        axis=1,
        keepdims=True,
    ).astype(I32)

    pl.semaphore_wait(barrier, line + plane - 2)

    def meta_copies(j):
        return [
            remote(src, metas.at[n, j], m_sem, (n, j), along(j))
            for n, src in enumerate((routes_ref, spots_ref))
        ]

    def query_copy(j):
        return remote(qline.at[0], qline.at[j], q_sem, (j,), along(j))

    def seat_copy(j, i):
        return remote(stage.at[j, i], got.at[:, j * plane + i], x_sem, (j, i), inside(i))

    def target_copy(i):
        return remote(zstage.at[i], zgot.at[i], t_sem, (i,), inside(i))

    def back_copy(j, i):
        return remote(dqs.at[:, j * plane + i], ret.at[j, i], r_sem, (j, i), inside(i))

    def part_copy(j):
        return remote(pstage.at[j], part.at[j], p_sem, (j,), along(j))

    for j in range(1, line):
        for copy in meta_copies(j):
            copy.start()

    for load in loads[3:6]:
        load.wait()
    pre = jnp.dot(features[...], w_hidden[...], preferred_element_type=F32)
    gate = 1.0 / (1.0 + jnp.exp(-pre))
    hidden[...] = (pre * gate).astype(BF16)
    slope[...] = gate * (1.0 + pre * (1.0 - gate))
    qline[0] = jnp.dot(hidden[...], w_out[...], preferred_element_type=F32).astype(BF16)
    for j in range(1, line):
        query_copy(j).start()

    lane = iota((1, LANES), 1)
    zstage[...] = jnp.zeros(zstage.shape, F32)

    def choose(j):
        routes = routes_ref if j == 0 else metas.at[0, j]
        spots = spots_ref if j == 0 else metas.at[1, j]
        target = jnp.zeros((hosted, users), F32)
        for r in range(visits):
            same = names == routes[r : r + 1, :]
            target = jnp.where(same, (spots[r : r + 1, :] + 1).astype(F32), target)
        member = target > 0.0
        rank = jnp.dot(flags(member), earlier[...], preferred_element_type=F32)
        code = jnp.where(member, rank, -1.0)
        codes[...] = code
        found = zstage[...].reshape(hosted, LANES)
        for s in range(cap):
            spot = jnp.sum(jnp.where(code == float(s), target, 0.0), axis=1, keepdims=True)
            found = jnp.where(lane == j * cap + s, spot, found)
        zstage[...] = found.reshape(plane, local_clusters, LANES)

        def block(i):
            own = codes[pl.ds(pl.multiple_of(i * local_clusters, TILE), local_clusters), :]
            if cap % TILE == 0:
                seat = iota((1, cap, 1), 1).astype(F32)
                chosen = flags((own[:, None, :] == seat).reshape(rows, users))
            else:
                first = iota((rows, local_clusters), 1) * cap
                row = iota((rows, local_clusters), 0)
                spread = flags((row >= first) & (row < first + cap))
                seat = (iota((rows, 1), 0) & (cap - 1)).astype(F32)
                wide = jnp.dot(spread, own.astype(BF16), preferred_element_type=F32)
                chosen = flags(wide == seat)
            sel[j, i] = chosen

        each(0, plane, block)

    def seated(j, i):
        value = jnp.dot(sel[j, i], qline[j], preferred_element_type=F32)
        return value.reshape(local_clusters, cap, width).astype(BF16)

    def send_seats(j):
        def block(i):
            stage[j, i] = seated(j, i)
            seat_copy(j, i).start()

        each(1, plane, block)
        got[:, j * plane] = seated(j, 0)

    choose(0)
    send_seats(0)
    for j in range(1, line):
        for copy in meta_copies(j):
            copy.wait_recv()
        choose(j)
    each(1, plane, lambda i: target_copy(i).start())
    zgot[0] = zstage[0]
    for j in range(1, line - 1):
        query_copy(j).wait_recv()
        send_seats(j)

    for load in loads[6:]:
        load.wait()
    for t in range(groups):
        here = slice(t * LANES, (t + 1) * LANES)
        count = counts[:, here]
        high = lax.shift_right_logical(count, 6)
        lookup[:, t, :] = ids[:, here].astype(F32)
        lookup[:, groups + t, :] = high.astype(F32)
        lookup[:, 2 * groups + t, :] = (count & 63).astype(F32)

    item = iota((item_rows, LANES), 0)
    step = 4
    for c in range(local_clusters):

        def weigh(t, total):
            for u in range(step):
                here = pl.ds(pl.multiple_of((t * step + u) * LANES, LANES), LANES)
                weight = 1.0 / counts[c : c + 1, here].astype(F32)
                total = total + jnp.where(ids[c : c + 1, here] == item, weight, 0.0)
            return total

        total = lax.fori_loop(0, groups // step, weigh, jnp.zeros((item_rows, LANES), F32))
        mass[c] = jnp.log(jnp.sum(total, axis=1, keepdims=True))

    query_copy(line - 1).wait_recv()
    send_seats(line - 1)

    features_t[...] = features[...].T
    each(1, plane, lambda i: target_copy(i).wait_recv())

    entry = iota((LANES, seats), 0)
    column = iota((LANES, seats), 1)
    source = lax.shift_right_logical(column, log2(cap))
    place = lax.shift_right_logical(source, log2(plane)) * cap + (column & (cap - 1))
    widen = flags(entry == place)
    from_row = lax.shift_right_logical(iota((hosted, seats), 0), log2(local_clusters))
    from_column = lax.shift_right_logical(iota((hosted, seats), 1), log2(cap)) & (plane - 1)
    matched = from_row == from_column
    fold = flags(
        iota((local_clusters, hosted), 0)
        == (iota((local_clusters, hosted), 1) & (local_clusters - 1))
    )
    z_all = zgot[...].reshape(hosted, LANES)
    z_high = jnp.floor(z_all * (1.0 / 64.0))
    z_low = z_all - z_high * 64.0

    def regroup(value):
        spread = jnp.dot(value.astype(BF16), widen, preferred_element_type=F32)
        spread = jnp.where(matched, spread, 0.0).astype(BF16)
        return jnp.dot(fold, spread, preferred_element_type=F32)

    spots_all = (regroup(z_high) * 64.0 + regroup(z_low)).astype(I32)
    for c in range(local_clusters):
        tpos[c] = spots_all[c : c + 1, :]

    for j in range(line):
        each(1, plane, lambda i: seat_copy(j, i).wait_recv())

    item_wide = iota((item_rows, seats), 0)
    low_wide = iota((LANES, seats), 0)
    high_wide = iota((groups, seats), 0)
    loss_lane = iota((1, loss_out.shape[1]), 1)

    def own(c, losses):
        query = got[c].reshape(seats, width)
        block = items[c]
        scores = lax.dot_general(
            block, query, (((1,), (1,)), ((), ())), preferred_element_type=F32
        )
        shifted = scores + mass[c]
        top = jnp.max(shifted, axis=0, keepdims=True)
        expo = jnp.exp(shifted - top)
        total = jnp.sum(expo, axis=0, keepdims=True)
        spot = tpos[c] - 1
        live = spot >= 0
        near = jnp.dot(
            lookup[c].astype(BF16),
            flags((spot & (LANES - 1)) == low_wide),
            preferred_element_type=F32,
        )
        here = lax.shift_right_logical(spot, log2(LANES)) == high_wide
        found = [
            jnp.sum(
                jnp.where(here, near[n * groups : (n + 1) * groups, :], 0.0), axis=0, keepdims=True
            )
            for n in range(3)
        ]
        own_id = jnp.where(live, found[0], -1.0).astype(I32)
        own_count = jnp.where(live, found[1] * 64.0 + found[2], 1.0)
        hit = own_id == item_wide
        picked = jnp.sum(jnp.where(hit, scores, 0.0), axis=0, keepdims=True) - jnp.log(own_count)
        loss = jnp.where(live, jnp.log(total) + top - picked, 0.0)
        mean = jnp.sum(loss, axis=1, keepdims=True) / jnp.sum(
            jnp.where(live, 1.0, 0.0), axis=1, keepdims=True
        )
        weight = (expo * (1.0 / total) - jnp.where(hit, 1.0, 0.0)).astype(BF16)
        wts[c] = weight
        dq = lax.dot_general(weight, block, (((0,), (0,)), ((), ())), preferred_element_type=F32)
        dqs[c] = dq.reshape(line * plane, cap, width).astype(BF16)
        return jnp.where(loss_lane == c, mean, losses)

    loss_out[...] = lax.fori_loop(0, local_clusters, own, jnp.zeros(loss_out.shape, F32))

    for j in range(line - 1, -1, -1):
        each(1, plane, lambda i: back_copy(j, i).start())
        ret[j, 0] = dqs[:, j * plane]

    def tables(c):
        table_out[c] = jnp.dot(
            wts[c], got[c].reshape(seats, width), preferred_element_type=F32
        )

    each(0, local_clusters, tables)

    def gather(j):
        each(1, plane, lambda i: back_copy(j, i).wait_recv())
        return lax.dot_general(
            sel[j].reshape(plane * rows, users),
            ret[j].reshape(plane * rows, width),
            (((0,), (0,)), ((), ())),
            preferred_element_type=F32,
        )

    for j in range(line - 1, 0, -1):
        pstage[j] = gather(j).astype(BF16)
        part_copy(j).start()
    total = gather(0)
    for j in range(1, line):
        part_copy(j).wait_recv()
        total = total + part[j].astype(F32)
    dq_total = total.astype(BF16)

    feat, hid = features.shape[1], hidden.shape[1]
    dhidden = lax.dot_general(
        dq_total, w_out[...], (((1,), (1,)), ((), ())), preferred_element_type=F32
    )
    dpre = (dhidden * slope[...]).astype(BF16)
    wide = 2 * LANES
    for b in range(hid // wide):
        product = jnp.dot(
            features_t[...], dpre[:, b * wide : (b + 1) * wide], preferred_element_type=F32
        )
        for h in range(2):
            acc[(2 * b + h) * feat : (2 * b + h + 1) * feat, :] = product[
                :, h * LANES : (h + 1) * LANES
            ]
    big_rows = feat * (hid // LANES)
    acc[big_rows : big_rows + hid, :] = lax.dot_general(
        hidden[...], dq_total, (((0,), (0,)), ((), ())), preferred_element_type=F32
    )
    if acc.shape[0] > big_rows + hid:
        spare = acc.shape[0] - big_rows - hid
        acc[big_rows + hid :, :] = jnp.zeros((spare, LANES), F32)

    chips = plane // 2
    core, chip = p % 2, p // 2
    units, a_units = split(line * plane, (feat + width) * hid)
    parts = line * chips * TILE
    a_len, b_len = a_units * parts, (units - a_units) * parts
    half = a_len + b_len
    a1_len, b1_len = a_len // chips, b_len // line
    a2_len, b2_len = a1_len // line, b1_len // chips
    base = core * half
    away = (1 - core) * half

    def at(start, size):
        return pl.ds(pl.multiple_of(start, TILE), size)

    def a_block(i):
        return base + flip(chip, i, chips) * a1_len

    def a_piece(i, j):
        return a_block(i) + flip(z, j, line) * a2_len

    def b_block(j):
        return base + a_len + flip(z, j, line) * b1_len

    def b_piece(j, i):
        return b_block(j) + flip(chip, i, chips) * b2_len

    started = []

    def give(start, size, inbox, sems, index, device):
        span = at(start, size)
        outb[span, :] = acc[span, :].astype(BF16)
        copy = remote(outb.at[span, :], inbox, sems, index, device)
        copy.start()
        started.append(copy)
        return copy

    def add(start, size, *arrived):
        span = at(start, size)
        total = acc[span, :]
        for inbox in arrived:
            total = total + inbox.astype(F32)
        acc[span, :] = total

    def chip_at(i):
        return inside(2 * i)

    core_a = give(away, a_len, core_in.at[0:a_len, :], c_sem, (0,), inside(1))
    core_b = give(away + a_len, b_len, core_in.at[a_len:half, :], c_sem, (1,), inside(1))
    core_a.wait_recv()
    add(base, a_len, core_in[0:a_len, :])
    a1 = [give(a_block(i), a1_len, a1_in.at[i], a1_sem, (i,), chip_at(i)) for i in range(1, chips)]
    core_b.wait_recv()
    add(base + a_len, b_len, core_in[a_len:half, :])
    b1 = [give(b_block(j), b1_len, b1_in.at[j], b1_sem, (j,), along(j)) for j in range(1, line)]
    for copy in a1:
        copy.wait_recv()
    add(a_block(0), a1_len, *[a1_in[i] for i in range(1, chips)])
    a2 = [give(a_piece(0, j), a2_len, a2_in.at[j], a2_sem, (j,), along(j)) for j in range(1, line)]
    for copy in b1:
        copy.wait_recv()
    add(b_block(0), b1_len, *[b1_in[j] for j in range(1, line)])
    b2 = [
        give(b_piece(0, i), b2_len, b2_in.at[i], b2_sem, (i,), chip_at(i)) for i in range(1, chips)
    ]

    def share(start, size, sems, index, device):
        span = at(start, size)
        copy = remote(full.at[span, :], full.at[span, :], sems, index, device)
        copy.start()
        started.append(copy)
        return copy

    def settle(start, size, *arrived):
        span = at(start, size)
        total = acc[span, :]
        for inbox in arrived:
            total = total + inbox.astype(F32)
        full[span, :] = total.astype(BF16)

    for copy in a2:
        copy.wait_recv()
    settle(a_piece(0, 0), a2_len, *[a2_in[j] for j in range(1, line)])
    az = [share(a_piece(0, 0), a2_len, az_sem, (j,), along(j)) for j in range(1, line)]
    ac = {}
    for i in range(1, chips):
        ac[i, 0] = share(a_piece(0, 0), a2_len, ac_sem, (i, 0), chip_at(i))
    for copy in b2:
        copy.wait_recv()
    settle(b_piece(0, 0), b2_len, *[b2_in[i] for i in range(1, chips)])
    bc = [share(b_piece(0, 0), b2_len, bc_sem, (i,), chip_at(i)) for i in range(1, chips)]
    bz = {}
    for j in range(1, line):
        bz[j, 0] = share(b_piece(0, 0), b2_len, bz_sem, (j, 0), along(j))
    for j in range(1, line):
        az[j - 1].wait_recv()
        for i in range(1, chips):
            ac[i, j] = share(a_piece(0, j), a2_len, ac_sem, (i, j), chip_at(i))
    ao = [share(a_block(0), a1_len, ao_sem, (0,), inside(1))]
    for i in range(1, chips):
        bc[i - 1].wait_recv()
        for j in range(1, line):
            bz[j, i] = share(b_piece(0, i), b2_len, bz_sem, (j, i), along(j))
    bo = [share(b_block(0), b1_len, bo_sem, (0,), inside(1))]
    for j in range(1, line):
        for i in range(chips):
            bz[j, i].wait_recv()
        bo.append(share(b_block(j), b1_len, bo_sem, (j,), inside(1)))
    for i in range(1, chips):
        for j in range(line):
            ac[i, j].wait_recv()
        ao.append(share(a_block(i), a1_len, ao_sem, (i,), inside(1)))
    for copy in ao + bo:
        copy.wait_recv()
    for b in range(hid // LANES):
        big_out[:, b * LANES : (b + 1) * LANES] = full[b * feat : (b + 1) * feat, :].astype(
            big_out.dtype
        )
    small_out[...] = full[big_rows : big_rows + hid, :].astype(small_out.dtype)

    for copy in started:
        copy.wait_send()
    for j in range(1, line):
        for copy in meta_copies(j) + [query_copy(j), part_copy(j)]:
            copy.wait_send()

    def sent(i):
        target_copy(i).wait_send()
        for j in range(line):
            seat_copy(j, i).wait_send()
            back_copy(j, i).wait_send()

    each(1, plane, sent)


def local(
    features, w_hidden, w_out, items, routes, cluster_slot, sample_ids, sample_counts, positives
):
    devices = lax.axis_size("dev")
    line, plane = LINE, devices // LINE
    chips = plane // 2
    users, visits = routes.shape
    feat, hid = w_hidden.shape
    width = w_out.shape[1]
    clusters = cluster_slot.shape[0]
    local_clusters, samples = sample_ids.shape
    item_rows = items.shape[0] // local_clusters
    cap = max(2, 2 * users * visits // (local_clusters * devices))
    rows = local_clusters * cap
    hosted = plane * local_clusters
    seats = devices * cap
    groups = samples // LANES
    units, a_units = split(devices, (feat + width) * hid)
    parts = line * chips * TILE
    a_len, b_len = a_units * parts, (units - a_units) * parts
    half = a_len + b_len
    vmem = pl.BlockSpec(memory_space=pltpu.VMEM)
    hbm = pl.BlockSpec(memory_space=pltpu.HBM)
    dma = pltpu.SemaphoreType.DMA
    loss, big, small, table = pl.pallas_call(
        functools.partial(step_kernel, line, plane, cap),
        out_shape=(
            jax.ShapeDtypeStruct((1, local_clusters), F32),
            jax.ShapeDtypeStruct((feat, hid), OUT),
            jax.ShapeDtypeStruct((hid, width), OUT),
            jax.ShapeDtypeStruct((local_clusters, item_rows, width), F32),
        ),
        in_specs=[hbm] * 9,
        out_specs=[vmem] * 4,
        scratch_shapes=[
            pltpu.VMEM((users, feat), BF16),
            pltpu.VMEM((feat, users), BF16),
            pltpu.VMEM((feat, hid), BF16),
            pltpu.VMEM((hid, width), BF16),
            pltpu.VMEM((local_clusters, item_rows, width), BF16),
            pltpu.VMEM((local_clusters, samples), I32),
            pltpu.VMEM((local_clusters, samples), I32),
            pltpu.VMEM((visits, users), I32),
            pltpu.VMEM((visits, users), I32),
            pltpu.VMEM((1, clusters), I32),
            pltpu.VMEM((users, hid), F32),
            pltpu.VMEM((users, hid), BF16),
            pltpu.VMEM((2, line, visits, users), I32),
            pltpu.VMEM((line, users, width), BF16),
            pltpu.VMEM((users, users), BF16),
            pltpu.VMEM((hosted, users), F32),
            pltpu.VMEM((line, plane, rows, users), BF16),
            pltpu.VMEM((line, plane, local_clusters, cap, width), BF16),
            pltpu.VMEM((local_clusters, devices, cap, width), BF16),
            pltpu.VMEM((plane, local_clusters, LANES), F32),
            pltpu.VMEM((plane, local_clusters, LANES), F32),
            pltpu.VMEM((local_clusters, 3 * groups, LANES), F32),
            pltpu.VMEM((local_clusters, item_rows, 1), F32),
            pltpu.VMEM((local_clusters, 1, seats), I32),
            pltpu.VMEM((local_clusters, item_rows, seats), BF16),
            pltpu.VMEM((local_clusters, devices, cap, width), BF16),
            pltpu.VMEM((line, plane, local_clusters, cap, width), BF16),
            pltpu.VMEM((line, users, width), BF16),
            pltpu.VMEM((line, users, width), BF16),
            pltpu.VMEM((2 * half, LANES), F32),
            pltpu.VMEM((2 * half, LANES), BF16),
            pltpu.VMEM((half, LANES), BF16),
            pltpu.VMEM((chips, a_len // chips, LANES), BF16),
            pltpu.VMEM((line, a_len // chips // line, LANES), BF16),
            pltpu.VMEM((line, b_len // line, LANES), BF16),
            pltpu.VMEM((chips, b_len // line // chips, LANES), BF16),
            pltpu.VMEM((2 * half, LANES), BF16),
            dma((9,)),
            dma((2, 2, line)),
            dma((2, line)),
            dma((2, line, plane)),
            dma((2, plane)),
            dma((2, line, plane)),
            dma((2, line)),
            dma((2, 2)),
            dma((2, chips)),
            dma((2, line)),
            dma((2, line)),
            dma((2, chips)),
            dma((2, line)),
            dma((2, chips, line)),
            dma((2, chips)),
            dma((2, line, chips)),
            dma((2, chips)),
            dma((2, line)),
        ],
        compiler_params=pltpu.CompilerParams(
            collective_id=0, has_side_effects=True, vmem_limit_bytes=VMEM_BYTES
        ),
        name="step",
    )(
        features,
        w_hidden,
        w_out,
        items.reshape(local_clusters, item_rows, width),
        sample_ids,
        sample_counts,
        routes.T,
        positives.T,
        cluster_slot.reshape(1, clusters),
    )
    return (
        loss.reshape(local_clusters),
        big.astype(F32),
        small.astype(F32),
        table.reshape(items.shape),
    )


OUT = BF16


def solution(mesh):
    in_specs = (
        P("dev", None),
        P(),
        P(),
        P("dev", None),
        P("dev", None),
        P(),
        P("dev", None),
        P("dev", None),
        P("dev", None),
    )
    out_specs = (P("dev"), P(), P(), P("dev", None))
    return jax.shard_map(local, mesh=mesh, in_specs=in_specs, out_specs=out_specs, check_vma=False)
```

```python
import functools

import jax
import jax.numpy as jnp
from jax import lax
from jax.experimental import pallas as pl
from jax.experimental.pallas import tpu as pltpu
from jax.sharding import PartitionSpec as P

LINE = 4
LANES = 128
TILE = 8
MESH = pl.DeviceIdType.MESH
F32, BF16, I32 = jnp.float32, jnp.bfloat16, jnp.int32
VMEM_BYTES = 48 * 1024 * 1024


def iota(shape, axis):
    return lax.broadcasted_iota(I32, shape, axis)


def flags(test):
    return jnp.where(test, 1.0, 0.0).astype(BF16)


def log2(value):
    return value.bit_length() - 1


def flip(index, other, size):
    result = index
    weight = 1
    while weight < size:
        mine = (index // weight) % 2
        theirs = (other // weight) % 2
        result = result + weight * (theirs - 2 * mine * theirs)
        weight *= 2
    return result


def each(low, high, action):
    def body(i, carry):
        action(i)
        return carry

    lax.fori_loop(low, high, body, 0)


def remote(src, dst, sems, at, device):
    return pltpu.make_async_remote_copy(
        src_ref=src,
        dst_ref=dst,
        send_sem=sems.at[(0,) + at],
        recv_sem=sems.at[(1,) + at],
        device_id=(device,),
        device_id_type=MESH,
    )


def summed_groups(line, chips, elements):
    parts = line * chips * TILE
    units = -(-(elements // LANES) // (2 * parts))
    pieces = 3
    groups = []
    start = 0
    for n in range(pieces):
        plane_first, share = True, (units + pieces - 1 - n) // pieces
        if share > 0:
            groups.append((plane_first, start, share * parts))
            start += share * parts
    return groups, start


def step_kernel(
    line,
    plane,
    cap,
    features_hbm,
    w_hidden_hbm,
    w_out_hbm,
    items_hbm,
    ids_hbm,
    counts_hbm,
    routes_hbm,
    spots_hbm,
    slot_hbm,
    loss_out,
    big_out,
    small_out,
    table_out,
    features,
    features_t,
    w_hidden,
    w_out,
    items,
    ids,
    counts,
    routes_ref,
    spots_ref,
    slot_ref,
    slope,
    hidden,
    metas,
    qline,
    earlier,
    codes,
    sel,
    stage,
    got,
    zstage,
    zgot,
    lookup,
    mass_left,
    mass_right,
    mass_grid,
    mass,
    tpos,
    own_item,
    own_count,
    wts,
    dqs,
    ret,
    pstage,
    part,
    acc,
    outb,
    core_in,
    inboxes,
    full,
    load_sem,
    m_sem,
    q_sem,
    x_sem,
    t_sem,
    r_sem,
    p_sem,
    c_sem,
    s1_sem,
    s2_sem,
    g1_sem,
    g2_sem,
    go_sem,
):
    me = lax.axis_index("dev")
    z, p = me // plane, me % plane

    def along(j):
        return flip(z, j, line) * plane + p

    def inside(i):
        return z * plane + flip(p, i, plane)

    visits, users = routes_ref.shape
    clusters = slot_ref.shape[1]
    local_clusters, samples = ids.shape
    item_rows, width = items.shape[1:]
    rows = local_clusters * cap
    hosted = plane * local_clusters
    seats = line * plane * cap
    groups = samples // LANES

    piece = users // 2
    top, bottom = pl.ds(0, piece), pl.ds(piece, piece)
    loads = [
        pltpu.make_async_copy(src, dst, load_sem.at[n])
        for n, (src, dst) in enumerate(
            [
                (w_hidden_hbm, w_hidden),
                (features_hbm.at[top, :], features.at[top, :]),
                (w_out_hbm, w_out),
                (features_hbm.at[bottom, :], features.at[bottom, :]),
                (routes_hbm, routes_ref),
                (spots_hbm, spots_ref),
                (slot_hbm, slot_ref),
                (ids_hbm, ids),
                (counts_hbm, counts),
                (items_hbm, items),
            ]
        )
    ]
    for load in loads:
        load.start()

    barrier = pltpu.get_barrier_semaphore()
    for j in range(1, line):
        pl.semaphore_signal(barrier, inc=1, device_id=(along(j),), device_id_type=MESH)
    each(
        1,
        plane,
        lambda i: pl.semaphore_signal(
            barrier, inc=1, device_id=(inside(i),), device_id_type=MESH
        ),
    )

    pl.semaphore_wait(barrier, line + plane - 2)

    def meta_copies(j):
        return [
            remote(src, metas.at[n, j], m_sem, (n, j), along(j))
            for n, src in enumerate((routes_ref, spots_ref))
        ]

    def half_copy(stock, arrived, sems, j, h, source, device):
        span = pl.ds(h * piece, piece)
        return remote(stock.at[source, span], arrived.at[j, span], sems, (j, h), device)

    def query_copy(j, h):
        source, device = (2, along(1)) if j == 3 else (0, along(j))
        return half_copy(qline, qline, q_sem, j, h, source, device)

    def seat_copy(j, i):
        return remote(stage.at[j, i], got.at[:, j * plane + i], x_sem, (j, i), inside(i))

    def target_copy(i):
        return remote(zstage.at[i], zgot.at[i], t_sem, (i,), inside(i))

    def back_copy(j, i):
        return remote(dqs.at[:, j * plane + i], ret.at[j, i], r_sem, (j, i), inside(i))

    def part_copy(j, h):
        return half_copy(pstage, part, p_sem, j, h, j, along(1 if j == 3 else j))

    for load in loads[0:3]:
        load.wait()
    for h in range(2):
        if h == 1:
            loads[3].wait()
        span = slice(h * piece, (h + 1) * piece)
        pre = jnp.dot(features[span, :], w_hidden[...], preferred_element_type=F32)
        gate = 1.0 / (1.0 + jnp.exp(-pre))
        active = (pre * gate).astype(BF16)
        hidden[span, :] = active
        slope[span, :] = pre
        qline[0, span, :] = jnp.dot(active, w_out[...], preferred_element_type=F32).astype(BF16)
        query_copy(2, h).start()
        query_copy(1, h).start()

    for load in loads[4:6]:
        load.wait()
    for j in range(1, line):
        for copy in meta_copies(j):
            copy.start()
    earlier[...] = flags(iota((users, users), 0) < iota((users, users), 1))
    loads[6].wait()
    k = iota((hosted, 1), 0)
    host = lax.bitwise_xor(lax.shift_right_logical(k, log2(local_clusters)), p)
    slot = (z * plane + host) * local_clusters + (k & (local_clusters - 1))
    names = jnp.sum(
        jnp.where(slot_ref[...] == slot, iota((hosted, clusters), 1), 0).astype(F32),
        axis=1,
        keepdims=True,
    ).astype(I32)

    lane = iota((1, LANES), 1)
    zstage[...] = jnp.zeros(zstage.shape, F32)

    def choose(j):
        routes = routes_ref if j == 0 else metas.at[0, j]
        spots = spots_ref if j == 0 else metas.at[1, j]
        target = jnp.zeros((hosted, users), F32)
        for r in range(visits):
            same = names == routes[r : r + 1, :]
            target = jnp.where(same, (spots[r : r + 1, :] + 1).astype(F32), target)
        member = target > 0.0
        rank = jnp.dot(flags(member), earlier[...], preferred_element_type=F32)
        code = jnp.where(member, rank, -1.0)
        codes[...] = code
        found = zstage[...].reshape(hosted, LANES)
        for s in range(cap):
            spot = jnp.sum(jnp.where(code == float(s), target, 0.0), axis=1, keepdims=True)
            found = jnp.where(lane == j * cap + s, spot, found)
        zstage[...] = found.reshape(plane, local_clusters, LANES)

        def block(i):
            own = codes[pl.ds(pl.multiple_of(i * local_clusters, TILE), local_clusters), :]
            if cap % TILE == 0:
                seat = iota((1, cap, 1), 1).astype(F32)
                chosen = flags((own[:, None, :] == seat).reshape(rows, users))
            else:
                first = iota((rows, local_clusters), 1) * cap
                row = iota((rows, local_clusters), 0)
                spread = flags((row >= first) & (row < first + cap))
                seat = (iota((rows, 1), 0) & (cap - 1)).astype(F32)
                wide = jnp.dot(spread, own.astype(BF16), preferred_element_type=F32)
                chosen = flags(wide == seat)
            sel[j, i] = chosen

        each(0, plane, block)

    def seated(j, i):
        value = jnp.dot(sel[j, i], qline[j], preferred_element_type=F32)
        return value.reshape(local_clusters, cap, width).astype(BF16)

    def send_seats(j):
        def block(i):
            stage[j, i] = seated(j, i)
            seat_copy(j, i).start()

        each(1, plane, block)
        got[:, j * plane] = seated(j, 0)

    def relay():
        for h in range(2):
            query_copy(2, h).wait_recv()
            query_copy(3, h).start()

    choose(0)
    send_seats(0)
    for j in range(1, line):
        for copy in meta_copies(j):
            copy.wait_recv()
        choose(j)
        if j == 2:
            relay()
    each(1, plane, lambda i: target_copy(i).start())
    zgot[0] = zstage[0]
    for h in range(2):
        query_copy(1, h).wait_recv()
    send_seats(1)
    send_seats(2)

    for load in loads[7:]:
        load.wait()
    for t in range(groups):
        here = slice(t * LANES, (t + 1) * LANES)
        count = counts[:, here]
        high = lax.shift_right_logical(count, 6)
        lookup[:, t, :] = ids[:, here].astype(F32)
        lookup[:, groups + t, :] = high.astype(F32)
        lookup[:, 2 * groups + t, :] = (count & 63).astype(F32)

    digit = 16
    tall = item_rows // digit
    chunk = mass_left.shape[1]
    mass_grid[...] = jnp.zeros(mass_grid.shape, F32)

    def weigh(t):
        here = pl.ds(pl.multiple_of(t * chunk, LANES), chunk)
        rest = 1.0 / counts[:, here].astype(F32)
        terms = []
        for _ in range(3):
            term = rest.astype(BF16).astype(F32)
            rest = rest - term
            terms.append(term)
        high = lax.shift_right_logical(ids[:, here], log2(digit))
        low = ids[:, here] & (digit - 1)
        for c in range(local_clusters):
            match = high[c : c + 1, :] == iota((tall, chunk), 0)
            mass_left[c * 3 * tall : (c + 1) * 3 * tall, :] = jnp.concatenate(
                [jnp.where(match, term[c : c + 1, :], 0.0) for term in terms], axis=0
            ).astype(BF16)
            mass_right[c * digit : (c + 1) * digit, :] = flags(
                low[c : c + 1, :] == iota((digit, chunk), 0)
            )
        mass_grid[...] += lax.dot_general(
            mass_left[...],
            mass_right[...],
            (((1,), (1,)), ((), ())),
            preferred_element_type=F32,
        )

    def settle_masses():
        across = local_clusters * digit
        column = iota((tall, across), 1)
        grid = jnp.zeros((tall, across), F32)
        for c in range(local_clusters):
            rows_c = mass_grid[c * 3 * tall : (c + 1) * 3 * tall, :]
            block = rows_c[0:tall] + rows_c[tall : 2 * tall] + rows_c[2 * tall : 3 * tall]
            grid = jnp.where(lax.shift_right_logical(column, log2(digit)) == c, block, grid)
        item = iota((item_rows, tall), 0)
        rise = jnp.where(
            lax.shift_right_logical(item, log2(digit)) == iota((item_rows, tall), 1), 1.0, 0.0
        )
        exact = lax.Precision.HIGHEST
        wide = jnp.dot(rise, grid, preferred_element_type=F32, precision=exact)
        same = (iota((item_rows, across), 0) & (digit - 1)) == (
            iota((item_rows, across), 1) & (digit - 1)
        )
        pick = jnp.where(
            lax.shift_right_logical(iota((across, local_clusters), 0), log2(digit))
            == iota((across, local_clusters), 1),
            1.0,
            0.0,
        )
        logs = jnp.log(
            jnp.dot(
                jnp.where(same, wide, 0.0), pick, preferred_element_type=F32, precision=exact
            )
        )
        for c in range(local_clusters):
            mass[c] = logs[:, c : c + 1]

    chunks = samples // chunk
    each(0, chunks // 2, weigh)
    for h in range(2):
        query_copy(3, h).wait_recv()
    send_seats(3)
    each(chunks // 2, chunks, weigh)
    settle_masses()
    pre = slope[...]
    gate = 1.0 / (1.0 + jnp.exp(-pre))
    slope[...] = gate * (1.0 + pre * (1.0 - gate))

    features_t[...] = features[...].T
    each(1, plane, lambda i: target_copy(i).wait_recv())

    entry = iota((LANES, seats), 0)
    column = iota((LANES, seats), 1)
    source = lax.shift_right_logical(column, log2(cap))
    place = lax.shift_right_logical(source, log2(plane)) * cap + (column & (cap - 1))
    widen = flags(entry == place)
    from_row = lax.shift_right_logical(iota((hosted, seats), 0), log2(local_clusters))
    from_column = lax.shift_right_logical(iota((hosted, seats), 1), log2(cap)) & (plane - 1)
    matched = from_row == from_column
    fold = flags(
        iota((local_clusters, hosted), 0)
        == (iota((local_clusters, hosted), 1) & (local_clusters - 1))
    )
    z_all = zgot[...].reshape(hosted, LANES)
    z_high = jnp.floor(z_all * (1.0 / 64.0))
    z_low = z_all - z_high * 64.0

    def regroup(value):
        spread = jnp.dot(value.astype(BF16), widen, preferred_element_type=F32)
        spread = jnp.where(matched, spread, 0.0).astype(BF16)
        return jnp.dot(fold, spread, preferred_element_type=F32)

    spots_all = (regroup(z_high) * 64.0 + regroup(z_low)).astype(I32)
    for c in range(local_clusters):
        tpos[c] = spots_all[c : c + 1, :]

    item_wide = iota((item_rows, seats), 0)
    low_wide = iota((LANES, seats), 0)
    high_wide = iota((groups, seats), 0)
    loss_lane = iota((1, loss_out.shape[1]), 1)
    together = 4

    def look_up(c):
        spot = tpos[c] - 1
        live = spot >= 0
        near = jnp.dot(
            lookup[c].astype(BF16),
            flags((spot & (LANES - 1)) == low_wide),
            preferred_element_type=F32,
        )
        here = lax.shift_right_logical(spot, log2(LANES)) == high_wide
        found = [
            jnp.sum(
                jnp.where(here, near[n * groups : (n + 1) * groups, :], 0.0), axis=0, keepdims=True
            )
            for n in range(3)
        ]
        own_item[c] = jnp.where(live, found[0], -1.0).astype(I32)
        own_count[c] = jnp.log(jnp.where(live, found[1] * 64.0 + found[2], 1.0))

    def look_up_some(n):
        for u in range(together):
            look_up(n * together + u)

    each(0, local_clusters // together, look_up_some)

    for j in range(line):
        each(1, plane, lambda i: seat_copy(j, i).wait_recv())

    def own(c, losses):
        query = got[c].reshape(seats, width)
        block = items[c]
        scores = lax.dot_general(
            block, query, (((1,), (1,)), ((), ())), preferred_element_type=F32
        )
        shifted = scores + mass[c]
        top = jnp.max(shifted, axis=0, keepdims=True)
        expo = jnp.exp(shifted - top)
        total = jnp.sum(expo, axis=0, keepdims=True)
        mine = own_item[c]
        live = jnp.where(mine >= 0, 1.0, 0.0)
        hit = mine == item_wide
        picked = jnp.sum(jnp.where(hit, scores, 0.0), axis=0, keepdims=True) - own_count[c]
        loss = (jnp.log(total) + top - picked) * live
        mean = jnp.sum(loss, axis=1, keepdims=True) / jnp.sum(live, axis=1, keepdims=True)
        weight = (expo * (1.0 / total) - jnp.where(hit, 1.0, 0.0)).astype(BF16)
        wts[c] = weight
        dq = lax.dot_general(weight, block, (((0,), (0,)), ((), ())), preferred_element_type=F32)
        dqs[c] = dq.reshape(line * plane, cap, width).astype(BF16)
        return jnp.where(loss_lane == c, mean, losses)

    def own_some(n, losses):
        for u in range(together):
            losses = own(n * together + u, losses)
        return losses

    loss_out[...] = lax.fori_loop(
        0, local_clusters // together, own_some, jnp.zeros(loss_out.shape, F32)
    )

    for j in range(line - 1, -1, -1):
        each(1, plane, lambda i: back_copy(j, i).start())
        ret[j, 0] = dqs[:, j * plane]

    def tables(c):
        table_out[c] = jnp.dot(
            wts[c], got[c].reshape(seats, width), preferred_element_type=F32
        )

    each(0, local_clusters, tables)

    def gather(j):
        each(1, plane, lambda i: back_copy(j, i).wait_recv())
        return lax.dot_general(
            sel[j].reshape(plane * rows, users),
            ret[j].reshape(plane * rows, width),
            (((0,), (0,)), ((), ())),
            preferred_element_type=F32,
        )

    def push(j, value):
        pstage[j] = value.astype(BF16)
        for h in range(2):
            part_copy(j, h).start()

    push(3, gather(3))
    second = gather(2)
    for h in range(2):
        span = slice(h * piece, (h + 1) * piece)
        part_copy(3, h).wait_recv()
        pstage[2, span, :] = (second[span, :] + part[3, span, :].astype(F32)).astype(BF16)
        part_copy(2, h).start()
    push(1, gather(1))
    total = gather(0)
    for j in (1, 2):
        for h in range(2):
            part_copy(j, h).wait_recv()
        total = total + part[j].astype(F32)
    dq_total = total.astype(BF16)

    feat, hid = features.shape[1], hidden.shape[1]
    dhidden = lax.dot_general(
        dq_total, w_out[...], (((1,), (1,)), ((), ())), preferred_element_type=F32
    )
    dpre = (dhidden * slope[...]).astype(BF16)
    wide = 2 * LANES
    for b in range(hid // wide):
        product = jnp.dot(
            features_t[...], dpre[:, b * wide : (b + 1) * wide], preferred_element_type=F32
        )
        for h in range(2):
            acc[(2 * b + h) * feat : (2 * b + h + 1) * feat, :] = product[
                :, h * LANES : (h + 1) * LANES
            ]
    big_rows = feat * (hid // LANES)
    acc[big_rows : big_rows + hid, :] = lax.dot_general(
        hidden[...], dq_total, (((0,), (0,)), ((), ())), preferred_element_type=F32
    )
    if acc.shape[0] > big_rows + hid:
        spare = acc.shape[0] - big_rows - hid
        acc[big_rows + hid :, :] = jnp.zeros((spare, LANES), F32)

    chips = plane // 2
    core, chip = p % 2, p // 2
    cuts, half = summed_groups(line, chips, (feat + width) * hid)
    base = core * half
    away = (1 - core) * half

    def at(start, size):
        return pl.ds(pl.multiple_of(start, TILE), size)

    class Cut:
        def __init__(self, n):
            self.n = n
            self.plane_first, self.start, self.size = cuts[n]
            self.count1, self.count2 = (chips, line) if self.plane_first else (line, chips)
            self.size1 = self.size // self.count1
            self.size2 = self.size1 // self.count2
            self.in1, self.in2 = inboxes[2 * n], inboxes[2 * n + 1]

        def device1(self, i):
            return inside(2 * i) if self.plane_first else along(i)

        def device2(self, i):
            return along(i) if self.plane_first else inside(2 * i)

        def block(self, i):
            mine = chip if self.plane_first else z
            return base + self.start + flip(mine, i, self.count1) * self.size1

        def piece(self, i, j):
            mine = z if self.plane_first else chip
            return self.block(i) + flip(mine, j, self.count2) * self.size2

    cut = [Cut(n) for n in range(len(cuts))]
    started = []

    def give(start, size, inbox, sems, index, device):
        span = at(start, size)
        outb[span, :] = acc[span, :].astype(BF16)
        copy = remote(outb.at[span, :], inbox, sems, index, device)
        copy.start()
        started.append(copy)
        return copy

    def added(start, size, arrived):
        total = acc[at(start, size), :]
        for inbox in arrived:
            total = total + inbox.astype(F32)
        return total

    def share(start, size, sems, index, device):
        span = at(start, size)
        copy = remote(full.at[span, :], full.at[span, :], sems, index, device)
        copy.start()
        started.append(copy)
        return copy

    def finish(copies):
        for copy in copies:
            copy.wait_recv()

    first = [
        give(away + c.start, c.size, core_in.at[c.start : c.start + c.size, :], c_sem, (c.n,), inside(1))
        for c in cut
    ]
    second = []
    for c in cut:
        first[c.n].wait_recv()
        mine = base + c.start
        acc[at(mine, c.size), :] = added(mine, c.size, [core_in[c.start : c.start + c.size, :]])
        second.append(
            [
                give(c.block(i), c.size1, c.in1.at[i], s1_sem, (c.n, i), c.device1(i))
                for i in range(1, c.count1)
            ]
        )
    third = []
    for c in cut:
        finish(second[c.n])
        acc[at(c.block(0), c.size1), :] = added(
            c.block(0), c.size1, [c.in1[i] for i in range(1, c.count1)]
        )
        third.append(
            [
                give(c.piece(0, j), c.size2, c.in2.at[j], s2_sem, (c.n, j), c.device2(j))
                for j in range(1, c.count2)
            ]
        )
    outer, inner, last = {}, {}, []
    for c in cut:
        finish(third[c.n])
        mine = c.piece(0, 0)
        full[at(mine, c.size2), :] = added(
            mine, c.size2, [c.in2[j] for j in range(1, c.count2)]
        ).astype(BF16)
        for j in range(1, c.count2):
            inner[c.n, j] = share(mine, c.size2, g2_sem, (c.n, j), c.device2(j))
        for i in range(1, c.count1):
            outer[c.n, i, 0] = share(mine, c.size2, g1_sem, (c.n, i, 0), c.device1(i))
    for c in cut:
        for j in range(1, c.count2):
            inner[c.n, j].wait_recv()
            for i in range(1, c.count1):
                outer[c.n, i, j] = share(
                    c.piece(0, j), c.size2, g1_sem, (c.n, i, j), c.device1(i)
                )
        last.append(share(c.block(0), c.size1, go_sem, (c.n, 0), inside(1)))
    for c in cut:
        for i in range(1, c.count1):
            finish(outer[c.n, i, j] for j in range(c.count2))
            last.append(share(c.block(i), c.size1, go_sem, (c.n, i), inside(1)))
    finish(last)
    for b in range(hid // LANES):
        big_out[:, b * LANES : (b + 1) * LANES] = full[b * feat : (b + 1) * feat, :].astype(
            big_out.dtype
        )
    small_out[...] = full[big_rows : big_rows + hid, :].astype(small_out.dtype)

    for copy in started:
        copy.wait_send()
    for j in range(1, line):
        for copy in meta_copies(j):
            copy.wait_send()
        for h in range(2):
            query_copy(j, h).wait_send()
            part_copy(j, h).wait_send()

    def sent(i):
        target_copy(i).wait_send()
        for j in range(line):
            seat_copy(j, i).wait_send()
            back_copy(j, i).wait_send()

    each(1, plane, sent)


def local(
    features, w_hidden, w_out, items, routes, cluster_slot, sample_ids, sample_counts, positives
):
    devices = lax.axis_size("dev")
    line, plane = LINE, devices // LINE
    chips = plane // 2
    users, visits = routes.shape
    feat, hid = w_hidden.shape
    width = w_out.shape[1]
    clusters = cluster_slot.shape[0]
    local_clusters, samples = sample_ids.shape
    item_rows = items.shape[0] // local_clusters
    cap = max(2, 2 * users * visits // (local_clusters * devices))
    rows = local_clusters * cap
    hosted = plane * local_clusters
    seats = devices * cap
    groups = samples // LANES
    cuts, half = summed_groups(line, chips, (feat + width) * hid)
    most = max(chips, line)
    inboxes = []
    for plane_first, _, size in cuts:
        count1, count2 = (chips, line) if plane_first else (line, chips)
        inboxes.append(pltpu.VMEM((count1, size // count1, LANES), BF16))
        inboxes.append(pltpu.VMEM((count2, size // count1 // count2, LANES), BF16))
    vmem = pl.BlockSpec(memory_space=pltpu.VMEM)
    hbm = pl.BlockSpec(memory_space=pltpu.HBM)
    dma = pltpu.SemaphoreType.DMA
    loss, big, small, table = pl.pallas_call(
        functools.partial(step_kernel, line, plane, cap),
        out_shape=(
            jax.ShapeDtypeStruct((1, local_clusters), F32),
            jax.ShapeDtypeStruct((feat, hid), OUT),
            jax.ShapeDtypeStruct((hid, width), OUT),
            jax.ShapeDtypeStruct((local_clusters, item_rows, width), F32),
        ),
        in_specs=[hbm] * 9,
        out_specs=[vmem] * 4,
        scratch_shapes=[
            pltpu.VMEM((users, feat), BF16),
            pltpu.VMEM((feat, users), BF16),
            pltpu.VMEM((feat, hid), BF16),
            pltpu.VMEM((hid, width), BF16),
            pltpu.VMEM((local_clusters, item_rows, width), BF16),
            pltpu.VMEM((local_clusters, samples), I32),
            pltpu.VMEM((local_clusters, samples), I32),
            pltpu.VMEM((visits, users), I32),
            pltpu.VMEM((visits, users), I32),
            pltpu.VMEM((1, clusters), I32),
            pltpu.VMEM((users, hid), F32),
            pltpu.VMEM((users, hid), BF16),
            pltpu.VMEM((2, line, visits, users), I32),
            pltpu.VMEM((line, users, width), BF16),
            pltpu.VMEM((users, users), BF16),
            pltpu.VMEM((hosted, users), F32),
            pltpu.VMEM((line, plane, rows, users), BF16),
            pltpu.VMEM((line, plane, local_clusters, cap, width), BF16),
            pltpu.VMEM((local_clusters, devices, cap, width), BF16),
            pltpu.VMEM((plane, local_clusters, LANES), F32),
            pltpu.VMEM((plane, local_clusters, LANES), F32),
            pltpu.VMEM((local_clusters, 3 * groups, LANES), F32),
            pltpu.VMEM((3 * local_clusters * (item_rows // 16), min(1024, samples)), BF16),
            pltpu.VMEM((16 * local_clusters, min(1024, samples)), BF16),
            pltpu.VMEM((3 * local_clusters * (item_rows // 16), 16 * local_clusters), F32),
            pltpu.VMEM((local_clusters, item_rows, 1), F32),
            pltpu.VMEM((local_clusters, 1, seats), I32),
            pltpu.VMEM((local_clusters, 1, seats), I32),
            pltpu.VMEM((local_clusters, 1, seats), F32),
            pltpu.VMEM((local_clusters, item_rows, seats), BF16),
            pltpu.VMEM((local_clusters, devices, cap, width), BF16),
            pltpu.VMEM((line, plane, local_clusters, cap, width), BF16),
            pltpu.VMEM((line, users, width), BF16),
            pltpu.VMEM((line, users, width), BF16),
            pltpu.VMEM((2 * half, LANES), F32),
            pltpu.VMEM((2 * half, LANES), BF16),
            pltpu.VMEM((half, LANES), BF16),
            inboxes,
            pltpu.VMEM((2 * half, LANES), BF16),
            dma((10,)),
            dma((2, 2, line)),
            dma((2, line, 2)),
            dma((2, line, plane)),
            dma((2, plane)),
            dma((2, line, plane)),
            dma((2, line, 2)),
            dma((2, len(cuts))),
            dma((2, len(cuts), most)),
            dma((2, len(cuts), most)),
            dma((2, len(cuts), most, most)),
            dma((2, len(cuts), most)),
            dma((2, len(cuts), most)),
        ],
        compiler_params=pltpu.CompilerParams(
            collective_id=0, has_side_effects=True, vmem_limit_bytes=VMEM_BYTES
        ),
        name="step",
    )(
        *(
            pltpu.with_memory_space_constraint(array, pltpu.HBM)
            for array in (
                features,
                w_hidden,
                w_out,
                items.reshape(local_clusters, item_rows, width),
                sample_ids,
                sample_counts,
                routes.T,
                positives.T,
                cluster_slot.reshape(1, clusters),
            )
        )
    )
    return finish(loss, big, small, table.reshape(items.shape))


def finish_kernel(loss_ref, big_ref, small_ref, table_ref, loss_out, big_out, small_out, table_out):
    loss_out[...] = loss_ref[...].reshape(loss_out.shape)
    big_out[...] = big_ref[...].astype(F32)
    small_out[...] = small_ref[...].astype(F32)
    table_out[...] = table_ref[...]


def finish(loss, big, small, table):
    steps = 4

    def cut(array):
        shape = array.shape
        return pl.BlockSpec((shape[0] // steps, shape[1]), lambda n: (n, 0))

    specs = [cut(big), cut(small), cut(table)]
    return pl.pallas_call(
        finish_kernel,
        grid=(steps,),
        out_shape=(
            jax.ShapeDtypeStruct(loss.shape[1:], F32),
            jax.ShapeDtypeStruct(big.shape, F32),
            jax.ShapeDtypeStruct(small.shape, F32),
            jax.ShapeDtypeStruct(table.shape, F32),
        ),
        in_specs=[pl.BlockSpec(loss.shape, lambda n: (0, 0))] + specs,
        out_specs=[pl.BlockSpec(loss.shape[1:], lambda n: (0,))] + specs,
        compiler_params=pltpu.CompilerParams(vmem_limit_bytes=VMEM_BYTES),
        name="finish",
    )(loss, big, small, table)


OUT = BF16


def solution(mesh):
    in_specs = (
        P("dev", None),
        P(),
        P(),
        P("dev", None),
        P("dev", None),
        P(),
        P("dev", None),
        P("dev", None),
        P("dev", None),
    )
    out_specs = (P("dev"), P(), P(), P("dev", None))
    return jax.shard_map(local, mesh=mesh, in_specs=in_specs, out_specs=out_specs, check_vma=False)
```

```python
import functools

import jax
import jax.numpy as jnp
from jax import lax
from jax.experimental import pallas as pl
from jax.experimental.pallas import tpu as pltpu
from jax.sharding import PartitionSpec as P

LINE = 4
LANES = 128
TILE = 8
MESH = pl.DeviceIdType.MESH
F32, BF16, I32 = jnp.float32, jnp.bfloat16, jnp.int32
VMEM_BYTES = 48 * 1024 * 1024


def iota(shape, axis):
    return lax.broadcasted_iota(I32, shape, axis)


def flags(test):
    return jnp.where(test, 1.0, 0.0).astype(BF16)


def log2(value):
    return value.bit_length() - 1


def flip(index, other, size):
    result = index
    weight = 1
    while weight < size:
        mine = (index // weight) % 2
        theirs = (other // weight) % 2
        result = result + weight * (theirs - 2 * mine * theirs)
        weight *= 2
    return result


def each(low, high, action):
    def body(i, carry):
        action(i)
        return carry

    lax.fori_loop(low, high, body, 0)


def remote(src, dst, sems, at, device):
    return pltpu.make_async_remote_copy(
        src_ref=src,
        dst_ref=dst,
        send_sem=sems.at[(0,) + at],
        recv_sem=sems.at[(1,) + at],
        device_id=(device,),
        device_id_type=MESH,
    )


def summed_groups(line, chips, elements):
    parts = line * chips * TILE
    units = -(-(elements // LANES) // (2 * parts))
    pieces = 3
    groups = []
    start = 0
    for n in range(pieces):
        plane_first, share = n % 2 == 0, (units + pieces - 1 - n) // pieces
        if share > 0:
            groups.append((plane_first, start, share * parts))
            start += share * parts
    return groups, start


def step_kernel(
    line,
    plane,
    cap,
    features_hbm,
    w_hidden_hbm,
    w_out_hbm,
    items_hbm,
    ids_hbm,
    counts_hbm,
    routes_hbm,
    spots_hbm,
    slot_hbm,
    loss_out,
    big_out,
    small_out,
    table_out,
    features,
    features_t,
    w_hidden,
    w_out,
    items,
    ids,
    counts,
    routes_ref,
    spots_ref,
    slot_ref,
    slope,
    hidden,
    metas,
    qline,
    earlier,
    codes,
    sel,
    stage,
    got,
    zstage,
    zgot,
    lookup,
    mass_left,
    mass_right,
    mass_grid,
    mass,
    tpos,
    own_item,
    own_count,
    wts,
    dqs,
    ret,
    pstage,
    part,
    acc,
    outb,
    core_in,
    inboxes,
    full,
    load_sem,
    m_sem,
    q_sem,
    x_sem,
    t_sem,
    r_sem,
    p_sem,
    c_sem,
    s1_sem,
    s2_sem,
    g1_sem,
    g2_sem,
    go_sem,
):
    me = lax.axis_index("dev")
    z, p = me // plane, me % plane

    def along(j):
        return flip(z, j, line) * plane + p

    def inside(i):
        return z * plane + flip(p, i, plane)

    visits, users = routes_ref.shape
    clusters = slot_ref.shape[1]
    local_clusters, samples = ids.shape
    item_rows, width = items.shape[1:]
    rows = local_clusters * cap
    hosted = plane * local_clusters
    seats = line * plane * cap
    groups = samples // LANES

    piece = users // 2
    top, bottom = pl.ds(0, piece), pl.ds(piece, piece)
    loads = [
        pltpu.make_async_copy(src, dst, load_sem.at[n])
        for n, (src, dst) in enumerate(
            [
                (w_hidden_hbm, w_hidden),
                (features_hbm.at[top, :], features.at[top, :]),
                (w_out_hbm, w_out),
                (features_hbm.at[bottom, :], features.at[bottom, :]),
                (routes_hbm, routes_ref),
                (spots_hbm, spots_ref),
                (slot_hbm, slot_ref),
                (ids_hbm, ids),
                (counts_hbm, counts),
                (items_hbm, items),
            ]
        )
    ]
    for load in loads:
        load.start()

    barrier = pltpu.get_barrier_semaphore()
    for j in range(1, line):
        pl.semaphore_signal(barrier, inc=1, device_id=(along(j),), device_id_type=MESH)
    each(
        1,
        plane,
        lambda i: pl.semaphore_signal(
            barrier, inc=1, device_id=(inside(i),), device_id_type=MESH
        ),
    )

    pl.semaphore_wait(barrier, line + plane - 2)

    def meta_copies(j):
        return [
            remote(src, metas.at[n, j], m_sem, (n, j), along(j))
            for n, src in enumerate((routes_ref, spots_ref))
        ]

    def half_copy(stock, arrived, sems, j, h, source, device):
        span = pl.ds(h * piece, piece)
        return remote(stock.at[source, span], arrived.at[j, span], sems, (j, h), device)

    def query_copy(j, h):
        source, device = (2, along(1)) if j == 3 else (0, along(j))
        return half_copy(qline, qline, q_sem, j, h, source, device)

    def seat_copy(j, i):
        return remote(stage.at[j, i], got.at[:, j * plane + i], x_sem, (j, i), inside(i))

    def target_copy(i):
        return remote(zstage.at[i], zgot.at[i], t_sem, (i,), inside(i))

    own_half = local_clusters // 2

    def back_copy(j, i, g):
        some = pl.ds(g * own_half, own_half)
        return remote(
            dqs.at[some, j * plane + i], ret.at[j, i, some], r_sem, (j, i, g), inside(i)
        )

    def back_copies(j, g):
        each(1, plane, lambda i: back_copy(j, i, g).start())

    def part_copy(j, h):
        return half_copy(pstage, part, p_sem, j, h, j, along(1 if j == 3 else j))

    for load in loads[0:3]:
        load.wait()
    for h in range(2):
        if h == 1:
            loads[3].wait()
        span = slice(h * piece, (h + 1) * piece)
        pre = jnp.dot(features[span, :], w_hidden[...], preferred_element_type=F32)
        gate = 1.0 / (1.0 + jnp.exp(-pre))
        active = (pre * gate).astype(BF16)
        hidden[span, :] = active
        slope[span, :] = pre
        qline[0, span, :] = jnp.dot(active, w_out[...], preferred_element_type=F32).astype(BF16)
        query_copy(2, h).start()
    for h in range(2):
        query_copy(1, h).start()

    for load in loads[4:6]:
        load.wait()
    for j in range(1, line):
        for copy in meta_copies(j):
            copy.start()
    earlier[...] = flags(iota((users, users), 0) < iota((users, users), 1))
    loads[6].wait()
    k = iota((hosted, 1), 0)
    host = lax.bitwise_xor(lax.shift_right_logical(k, log2(local_clusters)), p)
    slot = (z * plane + host) * local_clusters + (k & (local_clusters - 1))
    names = jnp.sum(
        jnp.where(slot_ref[...] == slot, iota((hosted, clusters), 1), 0).astype(F32),
        axis=1,
        keepdims=True,
    ).astype(I32)

    lane = iota((1, LANES), 1)
    zstage[...] = jnp.zeros(zstage.shape, F32)

    def choose(j):
        routes = routes_ref if j == 0 else metas.at[0, j]
        spots = spots_ref if j == 0 else metas.at[1, j]
        target = jnp.zeros((hosted, users), F32)
        for r in range(visits):
            same = names == routes[r : r + 1, :]
            target = jnp.where(same, (spots[r : r + 1, :] + 1).astype(F32), target)
        member = target > 0.0
        rank = jnp.dot(flags(member), earlier[...], preferred_element_type=F32)
        code = jnp.where(member, rank, -1.0)
        codes[...] = code
        found = zstage[...].reshape(hosted, LANES)
        for s in range(cap):
            spot = jnp.sum(jnp.where(code == float(s), target, 0.0), axis=1, keepdims=True)
            found = jnp.where(lane == j * cap + s, spot, found)
        zstage[...] = found.reshape(plane, local_clusters, LANES)

        def block(i):
            own = codes[pl.ds(pl.multiple_of(i * local_clusters, TILE), local_clusters), :]
            if cap % TILE == 0:
                seat = iota((1, cap, 1), 1).astype(F32)
                chosen = flags((own[:, None, :] == seat).reshape(rows, users))
            else:
                first = iota((rows, local_clusters), 1) * cap
                row = iota((rows, local_clusters), 0)
                spread = flags((row >= first) & (row < first + cap))
                seat = (iota((rows, 1), 0) & (cap - 1)).astype(F32)
                wide = jnp.dot(spread, own.astype(BF16), preferred_element_type=F32)
                chosen = flags(wide == seat)
            sel[j, i] = chosen

        each(0, plane, block)

    def seated(j, i):
        value = jnp.dot(sel[j, i], qline[j], preferred_element_type=F32)
        return value.reshape(local_clusters, cap, width).astype(BF16)

    def send_seats(j):
        def block(i):
            stage[j, i] = seated(j, i)
            seat_copy(j, i).start()

        each(1, plane, block)
        got[:, j * plane] = seated(j, 0)

    def relay():
        for h in range(2):
            query_copy(2, h).wait_recv()
            query_copy(3, h).start()

    choose(0)
    send_seats(0)
    for j in range(1, line):
        for copy in meta_copies(j):
            copy.wait_recv()
        choose(j)
        if j == 2:
            relay()
    each(1, plane, lambda i: target_copy(i).start())
    zgot[0] = zstage[0]
    for h in range(2):
        query_copy(1, h).wait_recv()
    send_seats(1)
    send_seats(2)

    for load in loads[7:]:
        load.wait()
    for t in range(groups):
        here = slice(t * LANES, (t + 1) * LANES)
        count = counts[:, here]
        high = lax.shift_right_logical(count, 6)
        lookup[:, t, :] = ids[:, here].astype(F32)
        lookup[:, groups + t, :] = high.astype(F32)
        lookup[:, 2 * groups + t, :] = (count & 63).astype(F32)

    digit = 16
    tall = item_rows // digit
    chunk = mass_left.shape[1]
    mass_grid[...] = jnp.zeros(mass_grid.shape, F32)

    def weigh(t):
        here = pl.ds(pl.multiple_of(t * chunk, LANES), chunk)
        rest = 1.0 / counts[:, here].astype(F32)
        terms = []
        for _ in range(3):
            term = rest.astype(BF16).astype(F32)
            rest = rest - term
            terms.append(term)
        high = lax.shift_right_logical(ids[:, here], log2(digit))
        low = ids[:, here] & (digit - 1)
        for c in range(local_clusters):
            match = high[c : c + 1, :] == iota((tall, chunk), 0)
            mass_left[c * 3 * tall : (c + 1) * 3 * tall, :] = jnp.concatenate(
                [jnp.where(match, term[c : c + 1, :], 0.0) for term in terms], axis=0
            ).astype(BF16)
            mass_right[c * digit : (c + 1) * digit, :] = flags(
                low[c : c + 1, :] == iota((digit, chunk), 0)
            )
        mass_grid[...] += lax.dot_general(
            mass_left[...],
            mass_right[...],
            (((1,), (1,)), ((), ())),
            preferred_element_type=F32,
        )

    def settle_masses():
        across = local_clusters * digit
        column = iota((tall, across), 1)
        grid = jnp.zeros((tall, across), F32)
        for c in range(local_clusters):
            rows_c = mass_grid[c * 3 * tall : (c + 1) * 3 * tall, :]
            block = rows_c[0:tall] + rows_c[tall : 2 * tall] + rows_c[2 * tall : 3 * tall]
            grid = jnp.where(lax.shift_right_logical(column, log2(digit)) == c, block, grid)
        item = iota((item_rows, tall), 0)
        rise = jnp.where(
            lax.shift_right_logical(item, log2(digit)) == iota((item_rows, tall), 1), 1.0, 0.0
        )
        exact = lax.Precision.HIGHEST
        wide = jnp.dot(rise, grid, preferred_element_type=F32, precision=exact)
        same = (iota((item_rows, across), 0) & (digit - 1)) == (
            iota((item_rows, across), 1) & (digit - 1)
        )
        pick = jnp.where(
            lax.shift_right_logical(iota((across, local_clusters), 0), log2(digit))
            == iota((across, local_clusters), 1),
            1.0,
            0.0,
        )
        logs = jnp.log(
            jnp.dot(
                jnp.where(same, wide, 0.0), pick, preferred_element_type=F32, precision=exact
            )
        )
        for c in range(local_clusters):
            mass[c] = logs[:, c : c + 1]

    chunks = samples // chunk
    each(0, chunks // 2, weigh)
    for h in range(2):
        query_copy(3, h).wait_recv()
    send_seats(3)
    each(chunks // 2, chunks, weigh)
    settle_masses()
    pre = slope[...]
    gate = 1.0 / (1.0 + jnp.exp(-pre))
    slope[...] = gate * (1.0 + pre * (1.0 - gate))

    features_t[...] = features[...].T
    each(1, plane, lambda i: target_copy(i).wait_recv())

    entry = iota((LANES, seats), 0)
    column = iota((LANES, seats), 1)
    source = lax.shift_right_logical(column, log2(cap))
    place = lax.shift_right_logical(source, log2(plane)) * cap + (column & (cap - 1))
    widen = flags(entry == place)
    from_row = lax.shift_right_logical(iota((hosted, seats), 0), log2(local_clusters))
    from_column = lax.shift_right_logical(iota((hosted, seats), 1), log2(cap)) & (plane - 1)
    matched = from_row == from_column
    fold = flags(
        iota((local_clusters, hosted), 0)
        == (iota((local_clusters, hosted), 1) & (local_clusters - 1))
    )
    z_all = zgot[...].reshape(hosted, LANES)
    z_high = jnp.floor(z_all * (1.0 / 64.0))
    z_low = z_all - z_high * 64.0

    def regroup(value):
        spread = jnp.dot(value.astype(BF16), widen, preferred_element_type=F32)
        spread = jnp.where(matched, spread, 0.0).astype(BF16)
        return jnp.dot(fold, spread, preferred_element_type=F32)

    spots_all = (regroup(z_high) * 64.0 + regroup(z_low)).astype(I32)
    for c in range(local_clusters):
        tpos[c] = spots_all[c : c + 1, :]

    item_wide = iota((item_rows, seats), 0)
    low_wide = iota((LANES, seats), 0)
    high_wide = iota((groups, seats), 0)
    loss_lane = iota((1, loss_out.shape[1]), 1)
    together = 4

    def look_up(c):
        spot = tpos[c] - 1
        live = spot >= 0
        near = jnp.dot(
            lookup[c].astype(BF16),
            flags((spot & (LANES - 1)) == low_wide),
            preferred_element_type=F32,
        )
        here = lax.shift_right_logical(spot, log2(LANES)) == high_wide
        found = [
            jnp.sum(
                jnp.where(here, near[n * groups : (n + 1) * groups, :], 0.0), axis=0, keepdims=True
            )
            for n in range(3)
        ]
        own_item[c] = jnp.where(live, found[0], -1.0).astype(I32)
        own_count[c] = jnp.log(jnp.where(live, found[1] * 64.0 + found[2], 1.0))

    def look_up_some(n):
        for u in range(together):
            look_up(n * together + u)

    each(0, local_clusters // together, look_up_some)

    for j in range(line):
        each(1, plane, lambda i: seat_copy(j, i).wait_recv())

    def own(c, losses):
        query = got[c].reshape(seats, width)
        block = items[c]
        scores = lax.dot_general(
            block, query, (((1,), (1,)), ((), ())), preferred_element_type=F32
        )
        shifted = scores + mass[c]
        top = jnp.max(shifted, axis=0, keepdims=True)
        expo = jnp.exp(shifted - top)
        total = jnp.sum(expo, axis=0, keepdims=True)
        mine = own_item[c]
        live = jnp.where(mine >= 0, 1.0, 0.0)
        hit = mine == item_wide
        picked = jnp.sum(jnp.where(hit, scores, 0.0), axis=0, keepdims=True) - own_count[c]
        loss = (jnp.log(total) + top - picked) * live
        mean = jnp.sum(loss, axis=1, keepdims=True) / jnp.sum(live, axis=1, keepdims=True)
        weight = (expo * (1.0 / total) - jnp.where(hit, 1.0, 0.0)).astype(BF16)
        wts[c] = weight
        dq = lax.dot_general(weight, block, (((0,), (0,)), ((), ())), preferred_element_type=F32)
        dqs[c] = dq.reshape(line * plane, cap, width).astype(BF16)
        return jnp.where(loss_lane == c, mean, losses)

    def own_some(n, losses):
        for u in range(together):
            losses = own(n * together + u, losses)
        return losses

    losses = lax.fori_loop(0, own_half // together, own_some, jnp.zeros(loss_out.shape, F32))
    for j in (3, 2):
        back_copies(j, 0)
    loss_out[...] = lax.fori_loop(
        own_half // together, local_clusters // together, own_some, losses
    )
    for j in (3, 2):
        back_copies(j, 1)
    for j in (1, 0):
        for g in range(2):
            back_copies(j, g)

    for j in range(line - 1, -1, -1):
        ret[j, 0] = dqs[:, j * plane]

    def tables(c):
        table_out[c] = jnp.dot(
            wts[c], got[c].reshape(seats, width), preferred_element_type=F32
        )

    each(0, local_clusters, tables)

    def gather(j):
        for g in range(2):
            each(1, plane, lambda i: back_copy(j, i, g).wait_recv())
        return lax.dot_general(
            sel[j].reshape(plane * rows, users),
            ret[j].reshape(plane * rows, width),
            (((0,), (0,)), ((), ())),
            preferred_element_type=F32,
        )

    def push(j, value):
        pstage[j] = value.astype(BF16)
        for h in range(2):
            part_copy(j, h).start()

    push(3, gather(3))
    second = gather(2)
    for h in range(2):
        span = slice(h * piece, (h + 1) * piece)
        part_copy(3, h).wait_recv()
        pstage[2, span, :] = (second[span, :] + part[3, span, :].astype(F32)).astype(BF16)
        part_copy(2, h).start()
    push(1, gather(1))
    total = gather(0)
    for j in (1, 2):
        for h in range(2):
            part_copy(j, h).wait_recv()
        total = total + part[j].astype(F32)
    dq_total = total.astype(BF16)

    feat, hid = features.shape[1], hidden.shape[1]
    dhidden = lax.dot_general(
        dq_total, w_out[...], (((1,), (1,)), ((), ())), preferred_element_type=F32
    )
    dpre = (dhidden * slope[...]).astype(BF16)
    wide = 2 * LANES
    for b in range(hid // wide):
        product = jnp.dot(
            features_t[...], dpre[:, b * wide : (b + 1) * wide], preferred_element_type=F32
        )
        for h in range(2):
            acc[(2 * b + h) * feat : (2 * b + h + 1) * feat, :] = product[
                :, h * LANES : (h + 1) * LANES
            ]
    big_rows = feat * (hid // LANES)
    acc[big_rows : big_rows + hid, :] = lax.dot_general(
        hidden[...], dq_total, (((0,), (0,)), ((), ())), preferred_element_type=F32
    )
    if acc.shape[0] > big_rows + hid:
        spare = acc.shape[0] - big_rows - hid
        acc[big_rows + hid :, :] = jnp.zeros((spare, LANES), F32)

    chips = plane // 2
    core, chip = p % 2, p // 2
    cuts, half = summed_groups(line, chips, (feat + width) * hid)
    base = core * half
    away = (1 - core) * half

    def at(start, size):
        return pl.ds(pl.multiple_of(start, TILE), size)

    class Cut:
        def __init__(self, n):
            self.n = n
            self.plane_first, self.start, self.size = cuts[n]
            self.count1, self.count2 = (chips, line) if self.plane_first else (line, chips)
            self.size1 = self.size // self.count1
            self.size2 = self.size1 // self.count2
            self.in1, self.in2 = inboxes[2 * n], inboxes[2 * n + 1]

        def device1(self, i):
            return inside(2 * i) if self.plane_first else along(i)

        def device2(self, i):
            return along(i) if self.plane_first else inside(2 * i)

        def block(self, i):
            mine = chip if self.plane_first else z
            return base + self.start + flip(mine, i, self.count1) * self.size1

        def piece(self, i, j):
            mine = z if self.plane_first else chip
            return self.block(i) + flip(mine, j, self.count2) * self.size2

    cut = [Cut(n) for n in range(len(cuts))]
    started = []

    def give(start, size, inbox, sems, index, device):
        span = at(start, size)
        outb[span, :] = acc[span, :].astype(BF16)
        copy = remote(outb.at[span, :], inbox, sems, index, device)
        copy.start()
        started.append(copy)
        return copy

    def added(start, size, arrived):
        total = acc[at(start, size), :]
        for inbox in arrived:
            total = total + inbox.astype(F32)
        return total

    def share(start, size, sems, index, device):
        span = at(start, size)
        copy = remote(full.at[span, :], full.at[span, :], sems, index, device)
        copy.start()
        started.append(copy)
        return copy

    def finish(copies):
        for copy in copies:
            copy.wait_recv()

    first = [
        give(away + c.start, c.size, core_in.at[c.start : c.start + c.size, :], c_sem, (c.n,), inside(1))
        for c in cut
    ]
    second = []
    for c in cut:
        first[c.n].wait_recv()
        mine = base + c.start
        acc[at(mine, c.size), :] = added(mine, c.size, [core_in[c.start : c.start + c.size, :]])
        second.append(
            [
                give(c.block(i), c.size1, c.in1.at[i], s1_sem, (c.n, i), c.device1(i))
                for i in range(1, c.count1)
            ]
        )
    third = []
    for c in cut:
        finish(second[c.n])
        acc[at(c.block(0), c.size1), :] = added(
            c.block(0), c.size1, [c.in1[i] for i in range(1, c.count1)]
        )
        third.append(
            [
                give(c.piece(0, j), c.size2, c.in2.at[j], s2_sem, (c.n, j), c.device2(j))
                for j in range(1, c.count2)
            ]
        )
    outer, inner, last = {}, {}, []
    for c in cut:
        finish(third[c.n])
        mine = c.piece(0, 0)
        full[at(mine, c.size2), :] = added(
            mine, c.size2, [c.in2[j] for j in range(1, c.count2)]
        ).astype(BF16)
        for j in range(1, c.count2):
            inner[c.n, j] = share(mine, c.size2, g2_sem, (c.n, j), c.device2(j))
        for i in range(1, c.count1):
            outer[c.n, i, 0] = share(mine, c.size2, g1_sem, (c.n, i, 0), c.device1(i))
    for c in cut:
        for j in range(1, c.count2):
            inner[c.n, j].wait_recv()
            for i in range(1, c.count1):
                outer[c.n, i, j] = share(
                    c.piece(0, j), c.size2, g1_sem, (c.n, i, j), c.device1(i)
                )
        last.append(share(c.block(0), c.size1, go_sem, (c.n, 0), inside(1)))
    for c in cut:
        for i in range(1, c.count1):
            finish(outer[c.n, i, j] for j in range(c.count2))
            last.append(share(c.block(i), c.size1, go_sem, (c.n, i), inside(1)))
    finish(last)
    for b in range(hid // LANES):
        big_out[:, b * LANES : (b + 1) * LANES] = full[b * feat : (b + 1) * feat, :].astype(
            big_out.dtype
        )
    small_out[...] = full[big_rows : big_rows + hid, :].astype(small_out.dtype)

    for copy in started:
        copy.wait_send()
    for j in range(1, line):
        for copy in meta_copies(j):
            copy.wait_send()
        for h in range(2):
            query_copy(j, h).wait_send()
            part_copy(j, h).wait_send()

    def sent(i):
        target_copy(i).wait_send()
        for j in range(line):
            seat_copy(j, i).wait_send()
            for g in range(2):
                back_copy(j, i, g).wait_send()

    each(1, plane, sent)


def local(
    features, w_hidden, w_out, items, routes, cluster_slot, sample_ids, sample_counts, positives
):
    devices = lax.axis_size("dev")
    line, plane = LINE, devices // LINE
    chips = plane // 2
    users, visits = routes.shape
    feat, hid = w_hidden.shape
    width = w_out.shape[1]
    clusters = cluster_slot.shape[0]
    local_clusters, samples = sample_ids.shape
    item_rows = items.shape[0] // local_clusters
    cap = max(2, 2 * users * visits // (local_clusters * devices))
    rows = local_clusters * cap
    hosted = plane * local_clusters
    seats = devices * cap
    groups = samples // LANES
    cuts, half = summed_groups(line, chips, (feat + width) * hid)
    most = max(chips, line)
    inboxes = []
    for plane_first, _, size in cuts:
        count1, count2 = (chips, line) if plane_first else (line, chips)
        inboxes.append(pltpu.VMEM((count1, size // count1, LANES), BF16))
        inboxes.append(pltpu.VMEM((count2, size // count1 // count2, LANES), BF16))
    vmem = pl.BlockSpec(memory_space=pltpu.VMEM)
    hbm = pl.BlockSpec(memory_space=pltpu.HBM)
    dma = pltpu.SemaphoreType.DMA
    loss, big, small, table = pl.pallas_call(
        functools.partial(step_kernel, line, plane, cap),
        out_shape=(
            jax.ShapeDtypeStruct((1, local_clusters), F32),
            jax.ShapeDtypeStruct((feat, hid), OUT),
            jax.ShapeDtypeStruct((hid, width), OUT),
            jax.ShapeDtypeStruct((local_clusters, item_rows, width), F32),
        ),
        in_specs=[hbm] * 9,
        out_specs=[vmem] * 4,
        scratch_shapes=[
            pltpu.VMEM((users, feat), BF16),
            pltpu.VMEM((feat, users), BF16),
            pltpu.VMEM((feat, hid), BF16),
            pltpu.VMEM((hid, width), BF16),
            pltpu.VMEM((local_clusters, item_rows, width), BF16),
            pltpu.VMEM((local_clusters, samples), I32),
            pltpu.VMEM((local_clusters, samples), I32),
            pltpu.VMEM((visits, users), I32),
            pltpu.VMEM((visits, users), I32),
            pltpu.VMEM((1, clusters), I32),
            pltpu.VMEM((users, hid), F32),
            pltpu.VMEM((users, hid), BF16),
            pltpu.VMEM((2, line, visits, users), I32),
            pltpu.VMEM((line, users, width), BF16),
            pltpu.VMEM((users, users), BF16),
            pltpu.VMEM((hosted, users), F32),
            pltpu.VMEM((line, plane, rows, users), BF16),
            pltpu.VMEM((line, plane, local_clusters, cap, width), BF16),
            pltpu.VMEM((local_clusters, devices, cap, width), BF16),
            pltpu.VMEM((plane, local_clusters, LANES), F32),
            pltpu.VMEM((plane, local_clusters, LANES), F32),
            pltpu.VMEM((local_clusters, 3 * groups, LANES), F32),
            pltpu.VMEM((3 * local_clusters * (item_rows // 16), min(1024, samples)), BF16),
            pltpu.VMEM((16 * local_clusters, min(1024, samples)), BF16),
            pltpu.VMEM((3 * local_clusters * (item_rows // 16), 16 * local_clusters), F32),
            pltpu.VMEM((local_clusters, item_rows, 1), F32),
            pltpu.VMEM((local_clusters, 1, seats), I32),
            pltpu.VMEM((local_clusters, 1, seats), I32),
            pltpu.VMEM((local_clusters, 1, seats), F32),
            pltpu.VMEM((local_clusters, item_rows, seats), BF16),
            pltpu.VMEM((local_clusters, devices, cap, width), BF16),
            pltpu.VMEM((line, plane, local_clusters, cap, width), BF16),
            pltpu.VMEM((line, users, width), BF16),
            pltpu.VMEM((line, users, width), BF16),
            pltpu.VMEM((2 * half, LANES), F32),
            pltpu.VMEM((2 * half, LANES), BF16),
            pltpu.VMEM((half, LANES), BF16),
            inboxes,
            pltpu.VMEM((2 * half, LANES), BF16),
            dma((10,)),
            dma((2, 2, line)),
            dma((2, line, 2)),
            dma((2, line, plane)),
            dma((2, plane)),
            dma((2, line, plane, 2)),
            dma((2, line, 2)),
            dma((2, len(cuts))),
            dma((2, len(cuts), most)),
            dma((2, len(cuts), most)),
            dma((2, len(cuts), most, most)),
            dma((2, len(cuts), most)),
            dma((2, len(cuts), most)),
        ],
        compiler_params=pltpu.CompilerParams(
            collective_id=0, has_side_effects=True, vmem_limit_bytes=VMEM_BYTES
        ),
        name="step",
    )(
        *(
            pltpu.with_memory_space_constraint(array, pltpu.HBM)
            for array in (
                features,
                w_hidden,
                w_out,
                items.reshape(local_clusters, item_rows, width),
                sample_ids,
                sample_counts,
                routes.T,
                positives.T,
                cluster_slot.reshape(1, clusters),
            )
        )
    )
    return finish(loss, big, small, table.reshape(items.shape))


def finish_kernel(loss_ref, big_ref, small_ref, table_ref, loss_out, big_out, small_out, table_out):
    loss_out[...] = loss_ref[...].reshape(loss_out.shape)
    big_out[...] = big_ref[...].astype(F32)
    small_out[...] = small_ref[...].astype(F32)
    table_out[...] = table_ref[...]


def finish(loss, big, small, table):
    steps = 4

    def cut(array):
        shape = array.shape
        return pl.BlockSpec((shape[0] // steps, shape[1]), lambda n: (n, 0))

    specs = [cut(big), cut(small), cut(table)]
    return pl.pallas_call(
        finish_kernel,
        grid=(steps,),
        out_shape=(
            jax.ShapeDtypeStruct(loss.shape[1:], F32),
            jax.ShapeDtypeStruct(big.shape, F32),
            jax.ShapeDtypeStruct(small.shape, F32),
            jax.ShapeDtypeStruct(table.shape, F32),
        ),
        in_specs=[pl.BlockSpec(loss.shape, lambda n: (0, 0))] + specs,
        out_specs=[pl.BlockSpec(loss.shape[1:], lambda n: (0,))] + specs,
        compiler_params=pltpu.CompilerParams(vmem_limit_bytes=VMEM_BYTES),
        name="finish",
    )(loss, big, small, table)


OUT = BF16


def solution(mesh):
    in_specs = (
        P("dev", None),
        P(),
        P(),
        P("dev", None),
        P("dev", None),
        P(),
        P("dev", None),
        P("dev", None),
        P("dev", None),
    )
    out_specs = (P("dev"), P(), P(), P("dev", None))
    return jax.shard_map(local, mesh=mesh, in_specs=in_specs, out_specs=out_specs, check_vma=False)
```

```python
import functools

import jax
import jax.numpy as jnp
from jax import lax
from jax.experimental import pallas as pl
from jax.experimental.pallas import tpu as pltpu
from jax.sharding import PartitionSpec as P

LINE = 4
LANES = 128
TILE = 8
MESH = pl.DeviceIdType.MESH
F32, BF16, I32 = jnp.float32, jnp.bfloat16, jnp.int32
VMEM_BYTES = 48 * 1024 * 1024


def iota(shape, axis):
    return lax.broadcasted_iota(I32, shape, axis)


def flags(test):
    return jnp.where(test, 1.0, 0.0).astype(BF16)


def log2(value):
    return value.bit_length() - 1


def flip(index, other, size):
    result = index
    weight = 1
    while weight < size:
        mine = (index // weight) % 2
        theirs = (other // weight) % 2
        result = result + weight * (theirs - 2 * mine * theirs)
        weight *= 2
    return result


def each(low, high, action):
    def body(i, carry):
        action(i)
        return carry

    lax.fori_loop(low, high, body, 0)


def remote(src, dst, sems, at, device):
    return pltpu.make_async_remote_copy(
        src_ref=src,
        dst_ref=dst,
        send_sem=sems.at[(0,) + at],
        recv_sem=sems.at[(1,) + at],
        device_id=(device,),
        device_id_type=MESH,
    )


def summed_groups(line, chips, elements):
    parts = line * chips * TILE
    units = -(-(elements // LANES) // (2 * parts))
    pieces = 3
    groups = []
    start = 0
    for n in range(pieces):
        plane_first, share = n % 2 == 0, (units + pieces - 1 - n) // pieces
        if share > 0:
            groups.append((plane_first, start, share * parts))
            start += share * parts
    return groups, start


def step_kernel(
    line,
    plane,
    cap,
    features_hbm,
    w_hidden_hbm,
    w_out_hbm,
    items_hbm,
    ids_hbm,
    counts_hbm,
    routes_hbm,
    spots_hbm,
    slot_hbm,
    loss_out,
    big_out,
    small_out,
    table_out,
    features,
    features_t,
    w_hidden,
    w_out,
    items,
    ids,
    counts,
    routes_ref,
    spots_ref,
    slot_ref,
    slope,
    hidden,
    metas,
    qline,
    earlier,
    codes,
    sel,
    stage,
    got,
    zstage,
    zgot,
    lookup,
    mass_left,
    mass_right,
    mass_grid,
    mass,
    tpos,
    own_item,
    own_count,
    wts,
    dqs,
    ret,
    pstage,
    part,
    acc,
    outb,
    core_in,
    inboxes,
    full,
    load_sem,
    m_sem,
    q_sem,
    x_sem,
    t_sem,
    r_sem,
    p_sem,
    c_sem,
    s1_sem,
    s2_sem,
    g1_sem,
    g2_sem,
    go_sem,
):
    me = lax.axis_index("dev")
    z, p = me // plane, me % plane

    def along(j):
        return flip(z, j, line) * plane + p

    def inside(i):
        return z * plane + flip(p, i, plane)

    visits, users = routes_ref.shape
    clusters = slot_ref.shape[1]
    local_clusters, samples = ids.shape
    item_rows, width = items.shape[1:]
    rows = local_clusters * cap
    hosted = plane * local_clusters
    seats = line * plane * cap
    groups = samples // LANES

    piece = users // 2
    top, bottom = pl.ds(0, piece), pl.ds(piece, piece)
    loads = [
        pltpu.make_async_copy(src, dst, load_sem.at[n])
        for n, (src, dst) in enumerate(
            [
                (w_hidden_hbm, w_hidden),
                (features_hbm.at[top, :], features.at[top, :]),
                (w_out_hbm, w_out),
                (features_hbm.at[bottom, :], features.at[bottom, :]),
                (routes_hbm, routes_ref),
                (spots_hbm, spots_ref),
                (slot_hbm, slot_ref),
                (ids_hbm, ids),
                (counts_hbm, counts),
                (items_hbm, items),
            ]
        )
    ]
    for load in loads:
        load.start()

    barrier = pltpu.get_barrier_semaphore()
    for j in range(1, line):
        pl.semaphore_signal(barrier, inc=1, device_id=(along(j),), device_id_type=MESH)
    each(
        1,
        plane,
        lambda i: pl.semaphore_signal(
            barrier, inc=1, device_id=(inside(i),), device_id_type=MESH
        ),
    )

    pl.semaphore_wait(barrier, line + plane - 2)

    def meta_copies(j):
        return [
            remote(src, metas.at[n, j], m_sem, (n, j), along(j))
            for n, src in enumerate((routes_ref, spots_ref))
        ]

    def half_copy(stock, arrived, sems, j, h, source, device):
        span = pl.ds(h * piece, piece)
        return remote(stock.at[source, span], arrived.at[j, span], sems, (j, h), device)

    def query_copy(j, h):
        source, device = (2, along(1)) if j == 3 else (0, along(j))
        return half_copy(qline, qline, q_sem, j, h, source, device)

    own_half = local_clusters // 2

    def seat_copy(j, i, g):
        some = pl.ds(g * own_half, own_half)
        return remote(
            stage.at[j, i, some], got.at[some, j * plane + i], x_sem, (j, i, g), inside(i)
        )

    def target_copy(i):
        return remote(zstage.at[i], zgot.at[i], t_sem, (i,), inside(i))

    def back_copy(j, i, g):
        some = pl.ds(g * own_half, own_half)
        return remote(
            dqs.at[some, j * plane + i], ret.at[j, i, some], r_sem, (j, i, g), inside(i)
        )

    def back_copies(j, g):
        each(1, plane, lambda i: back_copy(j, i, g).start())

    def part_copy(j, h):
        return half_copy(pstage, part, p_sem, j, h, j, along(1 if j == 3 else j))

    for load in loads[0:3]:
        load.wait()
    for h in range(2):
        if h == 1:
            loads[3].wait()
        span = slice(h * piece, (h + 1) * piece)
        pre = jnp.dot(features[span, :], w_hidden[...], preferred_element_type=F32)
        gate = 1.0 / (1.0 + jnp.exp(-pre))
        active = (pre * gate).astype(BF16)
        hidden[span, :] = active
        slope[span, :] = pre
        qline[0, span, :] = jnp.dot(active, w_out[...], preferred_element_type=F32).astype(BF16)
        query_copy(2, h).start()
    for h in range(2):
        query_copy(1, h).start()

    for load in loads[4:6]:
        load.wait()
    for j in range(1, line):
        for copy in meta_copies(j):
            copy.start()
    earlier[...] = flags(iota((users, users), 0) < iota((users, users), 1))
    loads[6].wait()
    k = iota((hosted, 1), 0)
    host = lax.bitwise_xor(lax.shift_right_logical(k, log2(local_clusters)), p)
    slot = (z * plane + host) * local_clusters + (k & (local_clusters - 1))
    names = jnp.sum(
        jnp.where(slot_ref[...] == slot, iota((hosted, clusters), 1), 0).astype(F32),
        axis=1,
        keepdims=True,
    ).astype(I32)

    lane = iota((1, LANES), 1)
    zstage[...] = jnp.zeros(zstage.shape, F32)

    def choose(j):
        routes = routes_ref if j == 0 else metas.at[0, j]
        spots = spots_ref if j == 0 else metas.at[1, j]
        target = jnp.zeros((hosted, users), F32)
        for r in range(visits):
            same = names == routes[r : r + 1, :]
            target = jnp.where(same, (spots[r : r + 1, :] + 1).astype(F32), target)
        member = target > 0.0
        rank = jnp.dot(flags(member), earlier[...], preferred_element_type=F32)
        code = jnp.where(member, rank, -1.0)
        codes[...] = code
        found = zstage[...].reshape(hosted, LANES)
        for s in range(cap):
            spot = jnp.sum(jnp.where(code == float(s), target, 0.0), axis=1, keepdims=True)
            found = jnp.where(lane == j * cap + s, spot, found)
        zstage[...] = found.reshape(plane, local_clusters, LANES)

        def block(i):
            own = codes[pl.ds(pl.multiple_of(i * local_clusters, TILE), local_clusters), :]
            if cap % TILE == 0:
                seat = iota((1, cap, 1), 1).astype(F32)
                chosen = flags((own[:, None, :] == seat).reshape(rows, users))
            else:
                first = iota((rows, local_clusters), 1) * cap
                row = iota((rows, local_clusters), 0)
                spread = flags((row >= first) & (row < first + cap))
                seat = (iota((rows, 1), 0) & (cap - 1)).astype(F32)
                wide = jnp.dot(spread, own.astype(BF16), preferred_element_type=F32)
                chosen = flags(wide == seat)
            sel[j, i] = chosen

        each(0, plane, block)

    def seated(j, i):
        value = jnp.dot(sel[j, i], qline[j], preferred_element_type=F32)
        return value.reshape(local_clusters, cap, width).astype(BF16)

    def send_seats(j):
        def block(i):
            stage[j, i] = seated(j, i)
            seat_copy(j, i, 0).start()
            if j < line - 1:
                seat_copy(j, i, 1).start()

        each(1, plane, block)
        if j == line - 1:
            each(1, plane, lambda i: seat_copy(j, i, 1).start())
        got[:, j * plane] = seated(j, 0)

    def relay():
        for h in range(2):
            query_copy(2, h).wait_recv()
            query_copy(3, h).start()

    choose(0)
    send_seats(0)
    for j in range(1, line):
        for copy in meta_copies(j):
            copy.wait_recv()
        choose(j)
        if j == 2:
            relay()
    each(1, plane, lambda i: target_copy(i).start())
    zgot[0] = zstage[0]
    for h in range(2):
        query_copy(1, h).wait_recv()
    send_seats(1)
    send_seats(2)

    for load in loads[7:]:
        load.wait()
    for t in range(groups):
        here = slice(t * LANES, (t + 1) * LANES)
        count = counts[:, here]
        high = lax.shift_right_logical(count, 6)
        lookup[:, t, :] = ids[:, here].astype(F32)
        lookup[:, groups + t, :] = high.astype(F32)
        lookup[:, 2 * groups + t, :] = (count & 63).astype(F32)

    digit = 16
    tall = item_rows // digit
    chunk = mass_left.shape[1]
    mass_grid[...] = jnp.zeros(mass_grid.shape, F32)

    def weigh(t):
        here = pl.ds(pl.multiple_of(t * chunk, LANES), chunk)
        rest = 1.0 / counts[:, here].astype(F32)
        terms = []
        for _ in range(3):
            term = rest.astype(BF16).astype(F32)
            rest = rest - term
            terms.append(term)
        high = lax.shift_right_logical(ids[:, here], log2(digit))
        low = ids[:, here] & (digit - 1)
        for c in range(local_clusters):
            match = high[c : c + 1, :] == iota((tall, chunk), 0)
            mass_left[c * 3 * tall : (c + 1) * 3 * tall, :] = jnp.concatenate(
                [jnp.where(match, term[c : c + 1, :], 0.0) for term in terms], axis=0
            ).astype(BF16)
            mass_right[c * digit : (c + 1) * digit, :] = flags(
                low[c : c + 1, :] == iota((digit, chunk), 0)
            )
        mass_grid[...] += lax.dot_general(
            mass_left[...],
            mass_right[...],
            (((1,), (1,)), ((), ())),
            preferred_element_type=F32,
        )

    def settle_masses():
        across = local_clusters * digit
        column = iota((tall, across), 1)
        grid = jnp.zeros((tall, across), F32)
        for c in range(local_clusters):
            rows_c = mass_grid[c * 3 * tall : (c + 1) * 3 * tall, :]
            block = rows_c[0:tall] + rows_c[tall : 2 * tall] + rows_c[2 * tall : 3 * tall]
            grid = jnp.where(lax.shift_right_logical(column, log2(digit)) == c, block, grid)
        item = iota((item_rows, tall), 0)
        rise = jnp.where(
            lax.shift_right_logical(item, log2(digit)) == iota((item_rows, tall), 1), 1.0, 0.0
        )
        exact = lax.Precision.HIGHEST
        wide = jnp.dot(rise, grid, preferred_element_type=F32, precision=exact)
        same = (iota((item_rows, across), 0) & (digit - 1)) == (
            iota((item_rows, across), 1) & (digit - 1)
        )
        pick = jnp.where(
            lax.shift_right_logical(iota((across, local_clusters), 0), log2(digit))
            == iota((across, local_clusters), 1),
            1.0,
            0.0,
        )
        logs = jnp.log(
            jnp.dot(
                jnp.where(same, wide, 0.0), pick, preferred_element_type=F32, precision=exact
            )
        )
        for c in range(local_clusters):
            mass[c] = logs[:, c : c + 1]

    chunks = samples // chunk
    each(0, chunks // 2, weigh)
    for h in range(2):
        query_copy(3, h).wait_recv()
    send_seats(3)
    each(chunks // 2, chunks, weigh)
    settle_masses()
    pre = slope[...]
    gate = 1.0 / (1.0 + jnp.exp(-pre))
    slope[...] = gate * (1.0 + pre * (1.0 - gate))

    features_t[...] = features[...].T
    each(1, plane, lambda i: target_copy(i).wait_recv())

    entry = iota((LANES, seats), 0)
    column = iota((LANES, seats), 1)
    source = lax.shift_right_logical(column, log2(cap))
    place = lax.shift_right_logical(source, log2(plane)) * cap + (column & (cap - 1))
    widen = flags(entry == place)
    from_row = lax.shift_right_logical(iota((hosted, seats), 0), log2(local_clusters))
    from_column = lax.shift_right_logical(iota((hosted, seats), 1), log2(cap)) & (plane - 1)
    matched = from_row == from_column
    fold = flags(
        iota((local_clusters, hosted), 0)
        == (iota((local_clusters, hosted), 1) & (local_clusters - 1))
    )
    z_all = zgot[...].reshape(hosted, LANES)
    z_high = jnp.floor(z_all * (1.0 / 64.0))
    z_low = z_all - z_high * 64.0

    def regroup(value):
        spread = jnp.dot(value.astype(BF16), widen, preferred_element_type=F32)
        spread = jnp.where(matched, spread, 0.0).astype(BF16)
        return jnp.dot(fold, spread, preferred_element_type=F32)

    spots_all = (regroup(z_high) * 64.0 + regroup(z_low)).astype(I32)
    for c in range(local_clusters):
        tpos[c] = spots_all[c : c + 1, :]

    item_wide = iota((item_rows, seats), 0)
    low_wide = iota((LANES, seats), 0)
    high_wide = iota((groups, seats), 0)
    loss_lane = iota((1, loss_out.shape[1]), 1)
    together = 4

    def look_up(c):
        spot = tpos[c] - 1
        live = spot >= 0
        near = jnp.dot(
            lookup[c].astype(BF16),
            flags((spot & (LANES - 1)) == low_wide),
            preferred_element_type=F32,
        )
        here = lax.shift_right_logical(spot, log2(LANES)) == high_wide
        found = [
            jnp.sum(
                jnp.where(here, near[n * groups : (n + 1) * groups, :], 0.0), axis=0, keepdims=True
            )
            for n in range(3)
        ]
        own_item[c] = jnp.where(live, found[0], -1.0).astype(I32)
        own_count[c] = jnp.log(jnp.where(live, found[1] * 64.0 + found[2], 1.0))

    def look_up_some(n):
        for u in range(together):
            look_up(n * together + u)

    each(0, local_clusters // together, look_up_some)

    for j in range(line):
        for g in range(1 if j == line - 1 else 2):
            each(1, plane, lambda i: seat_copy(j, i, g).wait_recv())

    def own(c, losses):
        query = got[c].reshape(seats, width)
        block = items[c]
        scores = lax.dot_general(
            block, query, (((1,), (1,)), ((), ())), preferred_element_type=F32
        )
        shifted = scores + mass[c]
        top = jnp.max(shifted, axis=0, keepdims=True)
        expo = jnp.exp(shifted - top)
        total = jnp.sum(expo, axis=0, keepdims=True)
        mine = own_item[c]
        live = jnp.where(mine >= 0, 1.0, 0.0)
        hit = mine == item_wide
        picked = jnp.sum(jnp.where(hit, scores, 0.0), axis=0, keepdims=True) - own_count[c]
        loss = (jnp.log(total) + top - picked) * live
        mean = jnp.sum(loss, axis=1, keepdims=True) / jnp.sum(live, axis=1, keepdims=True)
        weight = (expo * (1.0 / total) - jnp.where(hit, 1.0, 0.0)).astype(BF16)
        wts[c] = weight
        dq = lax.dot_general(weight, block, (((0,), (0,)), ((), ())), preferred_element_type=F32)
        dqs[c] = dq.reshape(line * plane, cap, width).astype(BF16)
        return jnp.where(loss_lane == c, mean, losses)

    def own_some(n, losses):
        for u in range(together):
            losses = own(n * together + u, losses)
        return losses

    losses = lax.fori_loop(0, own_half // together, own_some, jnp.zeros(loss_out.shape, F32))
    for j in (3, 2):
        back_copies(j, 0)
    each(1, plane, lambda i: seat_copy(line - 1, i, 1).wait_recv())
    loss_out[...] = lax.fori_loop(
        own_half // together, local_clusters // together, own_some, losses
    )
    for j in (3, 2):
        back_copies(j, 1)
    for j in (1, 0):
        for g in range(2):
            back_copies(j, g)

    for j in range(line - 1, -1, -1):
        ret[j, 0] = dqs[:, j * plane]

    def tables(c):
        table_out[c] = jnp.dot(
            wts[c], got[c].reshape(seats, width), preferred_element_type=F32
        )

    each(0, local_clusters, tables)

    for j in range(1, line):
        for copy in meta_copies(j):
            copy.wait_send()
        for h in range(2):
            query_copy(j, h).wait_send()

    def forward_sent(i):
        target_copy(i).wait_send()
        for j in range(line):
            for g in range(2):
                seat_copy(j, i, g).wait_send()

    each(1, plane, forward_sent)

    def gather(j):
        for g in range(2):
            each(1, plane, lambda i: back_copy(j, i, g).wait_recv())
        return lax.dot_general(
            sel[j].reshape(plane * rows, users),
            ret[j].reshape(plane * rows, width),
            (((0,), (0,)), ((), ())),
            preferred_element_type=F32,
        )

    def push(j, value):
        pstage[j] = value.astype(BF16)
        for h in range(2):
            part_copy(j, h).start()

    push(3, gather(3))
    second = gather(2)
    for h in range(2):
        span = slice(h * piece, (h + 1) * piece)
        part_copy(3, h).wait_recv()
        pstage[2, span, :] = (second[span, :] + part[3, span, :].astype(F32)).astype(BF16)
        part_copy(2, h).start()
    push(1, gather(1))
    total = gather(0)
    for j in (1, 2):
        for h in range(2):
            part_copy(j, h).wait_recv()
        total = total + part[j].astype(F32)
    dq_total = total.astype(BF16)

    feat, hid = features.shape[1], hidden.shape[1]
    dhidden = lax.dot_general(
        dq_total, w_out[...], (((1,), (1,)), ((), ())), preferred_element_type=F32
    )
    dpre = (dhidden * slope[...]).astype(BF16)
    wide = 2 * LANES
    for b in range(hid // wide):
        product = jnp.dot(
            features_t[...], dpre[:, b * wide : (b + 1) * wide], preferred_element_type=F32
        )
        for h in range(2):
            acc[(2 * b + h) * feat : (2 * b + h + 1) * feat, :] = product[
                :, h * LANES : (h + 1) * LANES
            ]
    big_rows = feat * (hid // LANES)
    acc[big_rows : big_rows + hid, :] = lax.dot_general(
        hidden[...], dq_total, (((0,), (0,)), ((), ())), preferred_element_type=F32
    )
    if acc.shape[0] > big_rows + hid:
        spare = acc.shape[0] - big_rows - hid
        acc[big_rows + hid :, :] = jnp.zeros((spare, LANES), F32)

    chips = plane // 2
    core, chip = p % 2, p // 2
    cuts, half = summed_groups(line, chips, (feat + width) * hid)
    base = core * half
    away = (1 - core) * half

    def at(start, size):
        return pl.ds(pl.multiple_of(start, TILE), size)

    class Cut:
        def __init__(self, n):
            self.n = n
            self.plane_first, self.start, self.size = cuts[n]
            self.count1, self.count2 = (chips, line) if self.plane_first else (line, chips)
            self.size1 = self.size // self.count1
            self.size2 = self.size1 // self.count2
            self.in1, self.in2 = inboxes[2 * n], inboxes[2 * n + 1]

        def device1(self, i):
            return inside(2 * i) if self.plane_first else along(i)

        def device2(self, i):
            return along(i) if self.plane_first else inside(2 * i)

        def block(self, i):
            mine = chip if self.plane_first else z
            return base + self.start + flip(mine, i, self.count1) * self.size1

        def piece(self, i, j):
            mine = z if self.plane_first else chip
            return self.block(i) + flip(mine, j, self.count2) * self.size2

    cut = [Cut(n) for n in range(len(cuts))]
    started = []

    def give(start, size, inbox, sems, index, device):
        span = at(start, size)
        outb[span, :] = acc[span, :].astype(BF16)
        copy = remote(outb.at[span, :], inbox, sems, index, device)
        copy.start()
        started.append(copy)
        return copy

    def added(start, size, arrived):
        total = acc[at(start, size), :]
        for inbox in arrived:
            total = total + inbox.astype(F32)
        return total

    def share(start, size, sems, index, device):
        span = at(start, size)
        copy = remote(full.at[span, :], full.at[span, :], sems, index, device)
        copy.start()
        started.append(copy)
        return copy

    def finish(copies):
        for copy in copies:
            copy.wait_recv()

    first = [
        give(away + c.start, c.size, core_in.at[c.start : c.start + c.size, :], c_sem, (c.n,), inside(1))
        for c in cut
    ]

    def backward_sent(i):
        for j in range(line):
            for g in range(2):
                back_copy(j, i, g).wait_send()

    each(1, plane, backward_sent)
    for j in range(1, line):
        for h in range(2):
            part_copy(j, h).wait_send()

    second = []
    for c in cut:
        first[c.n].wait_recv()
        mine = base + c.start
        acc[at(mine, c.size), :] = added(mine, c.size, [core_in[c.start : c.start + c.size, :]])
        second.append(
            [
                give(c.block(i), c.size1, c.in1.at[i], s1_sem, (c.n, i), c.device1(i))
                for i in range(1, c.count1)
            ]
        )
    third = []
    for c in cut:
        finish(second[c.n])
        acc[at(c.block(0), c.size1), :] = added(
            c.block(0), c.size1, [c.in1[i] for i in range(1, c.count1)]
        )
        third.append(
            [
                give(c.piece(0, j), c.size2, c.in2.at[j], s2_sem, (c.n, j), c.device2(j))
                for j in range(1, c.count2)
            ]
        )
    outer, inner, last = {}, {}, []
    for c in cut:
        finish(third[c.n])
        mine = c.piece(0, 0)
        full[at(mine, c.size2), :] = added(
            mine, c.size2, [c.in2[j] for j in range(1, c.count2)]
        ).astype(BF16)
        for j in range(1, c.count2):
            inner[c.n, j] = share(mine, c.size2, g2_sem, (c.n, j), c.device2(j))
        for i in range(1, c.count1):
            outer[c.n, i, 0] = share(mine, c.size2, g1_sem, (c.n, i, 0), c.device1(i))
    for c in cut:
        for j in range(1, c.count2):
            inner[c.n, j].wait_recv()
            for i in range(1, c.count1):
                outer[c.n, i, j] = share(
                    c.piece(0, j), c.size2, g1_sem, (c.n, i, j), c.device1(i)
                )
        last.append(share(c.block(0), c.size1, go_sem, (c.n, 0), inside(1)))
    for c in cut:
        for i in range(1, c.count1):
            finish(outer[c.n, i, j] for j in range(c.count2))
            last.append(share(c.block(i), c.size1, go_sem, (c.n, i), inside(1)))
    finish(last)
    for b in range(hid // LANES):
        big_out[:, b * LANES : (b + 1) * LANES] = full[b * feat : (b + 1) * feat, :].astype(
            big_out.dtype
        )
    small_out[...] = full[big_rows : big_rows + hid, :].astype(small_out.dtype)

    for copy in started:
        copy.wait_send()


def local(
    features, w_hidden, w_out, items, routes, cluster_slot, sample_ids, sample_counts, positives
):
    devices = lax.axis_size("dev")
    line, plane = LINE, devices // LINE
    chips = plane // 2
    users, visits = routes.shape
    feat, hid = w_hidden.shape
    width = w_out.shape[1]
    clusters = cluster_slot.shape[0]
    local_clusters, samples = sample_ids.shape
    item_rows = items.shape[0] // local_clusters
    cap = max(2, 2 * users * visits // (local_clusters * devices))
    rows = local_clusters * cap
    hosted = plane * local_clusters
    seats = devices * cap
    groups = samples // LANES
    cuts, half = summed_groups(line, chips, (feat + width) * hid)
    most = max(chips, line)
    inboxes = []
    for plane_first, _, size in cuts:
        count1, count2 = (chips, line) if plane_first else (line, chips)
        inboxes.append(pltpu.VMEM((count1, size // count1, LANES), BF16))
        inboxes.append(pltpu.VMEM((count2, size // count1 // count2, LANES), BF16))
    vmem = pl.BlockSpec(memory_space=pltpu.VMEM)
    hbm = pl.BlockSpec(memory_space=pltpu.HBM)
    dma = pltpu.SemaphoreType.DMA
    loss, big, small, table = pl.pallas_call(
        functools.partial(step_kernel, line, plane, cap),
        out_shape=(
            jax.ShapeDtypeStruct((1, local_clusters), F32),
            jax.ShapeDtypeStruct((feat, hid), OUT),
            jax.ShapeDtypeStruct((hid, width), OUT),
            jax.ShapeDtypeStruct((local_clusters, item_rows, width), F32),
        ),
        in_specs=[hbm] * 9,
        out_specs=[vmem] * 4,
        scratch_shapes=[
            pltpu.VMEM((users, feat), BF16),
            pltpu.VMEM((feat, users), BF16),
            pltpu.VMEM((feat, hid), BF16),
            pltpu.VMEM((hid, width), BF16),
            pltpu.VMEM((local_clusters, item_rows, width), BF16),
            pltpu.VMEM((local_clusters, samples), I32),
            pltpu.VMEM((local_clusters, samples), I32),
            pltpu.VMEM((visits, users), I32),
            pltpu.VMEM((visits, users), I32),
            pltpu.VMEM((1, clusters), I32),
            pltpu.VMEM((users, hid), F32),
            pltpu.VMEM((users, hid), BF16),
            pltpu.VMEM((2, line, visits, users), I32),
            pltpu.VMEM((line, users, width), BF16),
            pltpu.VMEM((users, users), BF16),
            pltpu.VMEM((hosted, users), F32),
            pltpu.VMEM((line, plane, rows, users), BF16),
            pltpu.VMEM((line, plane, local_clusters, cap, width), BF16),
            pltpu.VMEM((local_clusters, devices, cap, width), BF16),
            pltpu.VMEM((plane, local_clusters, LANES), F32),
            pltpu.VMEM((plane, local_clusters, LANES), F32),
            pltpu.VMEM((local_clusters, 3 * groups, LANES), F32),
            pltpu.VMEM((3 * local_clusters * (item_rows // 16), min(1024, samples)), BF16),
            pltpu.VMEM((16 * local_clusters, min(1024, samples)), BF16),
            pltpu.VMEM((3 * local_clusters * (item_rows // 16), 16 * local_clusters), F32),
            pltpu.VMEM((local_clusters, item_rows, 1), F32),
            pltpu.VMEM((local_clusters, 1, seats), I32),
            pltpu.VMEM((local_clusters, 1, seats), I32),
            pltpu.VMEM((local_clusters, 1, seats), F32),
            pltpu.VMEM((local_clusters, item_rows, seats), BF16),
            pltpu.VMEM((local_clusters, devices, cap, width), BF16),
            pltpu.VMEM((line, plane, local_clusters, cap, width), BF16),
            pltpu.VMEM((line, users, width), BF16),
            pltpu.VMEM((line, users, width), BF16),
            pltpu.VMEM((2 * half, LANES), F32),
            pltpu.VMEM((2 * half, LANES), BF16),
            pltpu.VMEM((half, LANES), BF16),
            inboxes,
            pltpu.VMEM((2 * half, LANES), BF16),
            dma((10,)),
            dma((2, 2, line)),
            dma((2, line, 2)),
            dma((2, line, plane, 2)),
            dma((2, plane)),
            dma((2, line, plane, 2)),
            dma((2, line, 2)),
            dma((2, len(cuts))),
            dma((2, len(cuts), most)),
            dma((2, len(cuts), most)),
            dma((2, len(cuts), most, most)),
            dma((2, len(cuts), most)),
            dma((2, len(cuts), most)),
        ],
        compiler_params=pltpu.CompilerParams(
            collective_id=0, has_side_effects=True, vmem_limit_bytes=VMEM_BYTES
        ),
        name="step",
    )(
        *(
            pltpu.with_memory_space_constraint(array, pltpu.HBM)
            for array in (
                features,
                w_hidden,
                w_out,
                items.reshape(local_clusters, item_rows, width),
                sample_ids,
                sample_counts,
                routes.T,
                positives.T,
                cluster_slot.reshape(1, clusters),
            )
        )
    )
    return finish(loss, big, small, table.reshape(items.shape))


def finish_kernel(loss_ref, big_ref, small_ref, table_ref, loss_out, big_out, small_out, table_out):
    loss_out[...] = loss_ref[...].reshape(loss_out.shape)
    big_out[...] = big_ref[...].astype(F32)
    small_out[...] = small_ref[...].astype(F32)
    table_out[...] = table_ref[...]


def finish(loss, big, small, table):
    steps = 2

    def cut(array):
        shape = array.shape
        return pl.BlockSpec((shape[0] // steps, shape[1]), lambda n: (n, 0))

    specs = [cut(big), cut(small), cut(table)]
    return pl.pallas_call(
        finish_kernel,
        grid=(steps,),
        out_shape=(
            jax.ShapeDtypeStruct(loss.shape[1:], F32),
            jax.ShapeDtypeStruct(big.shape, F32),
            jax.ShapeDtypeStruct(small.shape, F32),
            jax.ShapeDtypeStruct(table.shape, F32),
        ),
        in_specs=[pl.BlockSpec(loss.shape, lambda n: (0, 0))] + specs,
        out_specs=[pl.BlockSpec(loss.shape[1:], lambda n: (0,))] + specs,
        compiler_params=pltpu.CompilerParams(vmem_limit_bytes=VMEM_BYTES),
        name="finish",
    )(loss, big, small, table)


OUT = BF16


def solution(mesh):
    in_specs = (
        P("dev", None),
        P(),
        P(),
        P("dev", None),
        P("dev", None),
        P(),
        P("dev", None),
        P("dev", None),
        P("dev", None),
    )
    out_specs = (P("dev"), P(), P(), P("dev", None))
    return jax.shard_map(local, mesh=mesh, in_specs=in_specs, out_specs=out_specs, check_vma=False)
```

```python
import functools

import jax
import jax.numpy as jnp
from jax import lax
from jax.experimental import pallas as pl
from jax.experimental.pallas import tpu as pltpu
from jax.sharding import PartitionSpec as P

LINE = 4
LANES = 128
TILE = 8
MESH = pl.DeviceIdType.MESH
F32, BF16, I32 = jnp.float32, jnp.bfloat16, jnp.int32
VMEM_BYTES = 48 * 1024 * 1024


def iota(shape, axis):
    return lax.broadcasted_iota(I32, shape, axis)


def flags(test):
    return jnp.where(test, 1.0, 0.0).astype(BF16)


def log2(value):
    return value.bit_length() - 1


def flip(index, other, size):
    result = index
    weight = 1
    while weight < size:
        mine = (index // weight) % 2
        theirs = (other // weight) % 2
        result = result + weight * (theirs - 2 * mine * theirs)
        weight *= 2
    return result


def each(low, high, action):
    def body(i, carry):
        action(i)
        return carry

    lax.fori_loop(low, high, body, 0)


def remote(src, dst, sems, at, device):
    return pltpu.make_async_remote_copy(
        src_ref=src,
        dst_ref=dst,
        send_sem=sems.at[(0,) + at],
        recv_sem=sems.at[(1,) + at],
        device_id=(device,),
        device_id_type=MESH,
    )


def summed_groups(line, chips, elements):
    parts = line * chips * TILE
    units = -(-(elements // LANES) // (2 * parts))
    pieces = 3
    groups = []
    start = 0
    for n in range(pieces):
        plane_first, share = n % 2 == 0, (units + pieces - 1 - n) // pieces
        if share > 0:
            groups.append((plane_first, start, share * parts))
            start += share * parts
    return groups, start


def step_kernel(
    line,
    plane,
    cap,
    features_hbm,
    w_hidden_hbm,
    w_out_hbm,
    items_hbm,
    ids_hbm,
    counts_hbm,
    routes_hbm,
    spots_hbm,
    slot_hbm,
    loss_out,
    big_out,
    small_out,
    table_out,
    features,
    features_t,
    w_hidden,
    w_out,
    items,
    ids,
    counts,
    routes_ref,
    spots_ref,
    slot_ref,
    slope,
    hidden,
    metas,
    qline,
    earlier,
    codes,
    sel,
    stage,
    got,
    zstage,
    zgot,
    lookup,
    mass_left,
    mass_right,
    mass_grid,
    mass,
    tpos,
    own_item,
    own_count,
    wts,
    dqs,
    ret,
    pstage,
    part,
    acc,
    outb,
    core_in,
    inboxes,
    full,
    load_sem,
    m_sem,
    q_sem,
    x_sem,
    t_sem,
    r_sem,
    p_sem,
    c_sem,
    s1_sem,
    s2_sem,
    g1_sem,
    g2_sem,
    go_sem,
):
    me = lax.axis_index("dev")
    z, p = me // plane, me % plane

    def along(j):
        return flip(z, j, line) * plane + p

    def inside(i):
        return z * plane + flip(p, i, plane)

    visits, users = routes_ref.shape
    clusters = slot_ref.shape[1]
    local_clusters, samples = ids.shape
    item_rows, width = items.shape[1:]
    rows = local_clusters * cap
    hosted = plane * local_clusters
    seats = line * plane * cap
    groups = samples // LANES

    piece = users // 2
    top, bottom = pl.ds(0, piece), pl.ds(piece, piece)
    loads = [
        pltpu.make_async_copy(src, dst, load_sem.at[n])
        for n, (src, dst) in enumerate(
            [
                (w_hidden_hbm, w_hidden),
                (features_hbm.at[top, :], features.at[top, :]),
                (w_out_hbm, w_out),
                (features_hbm.at[bottom, :], features.at[bottom, :]),
                (routes_hbm, routes_ref),
                (spots_hbm, spots_ref),
                (slot_hbm, slot_ref),
                (ids_hbm, ids),
                (counts_hbm, counts),
                (items_hbm, items),
            ]
        )
    ]
    for load in loads:
        load.start()

    barrier = pltpu.get_barrier_semaphore()
    for j in range(1, line):
        pl.semaphore_signal(barrier, inc=1, device_id=(along(j),), device_id_type=MESH)
    each(
        1,
        plane,
        lambda i: pl.semaphore_signal(
            barrier, inc=1, device_id=(inside(i),), device_id_type=MESH
        ),
    )

    pl.semaphore_wait(barrier, line + plane - 2)

    def meta_copies(j):
        return [
            remote(src, metas.at[n, j], m_sem, (n, j), along(j))
            for n, src in enumerate((routes_ref, spots_ref))
        ]

    def half_copy(stock, arrived, sems, j, h, source, device):
        span = pl.ds(h * piece, piece)
        return remote(stock.at[source, span], arrived.at[j, span], sems, (j, h), device)

    def query_copy(j, h):
        source, device = (2, along(1)) if j == 3 else (0, along(j))
        return half_copy(qline, qline, q_sem, j, h, source, device)

    own_half = local_clusters // 2

    def seat_copy(j, i, g):
        some = pl.ds(g * own_half, own_half)
        return remote(
            stage.at[j, i, some], got.at[some, j * plane + i], x_sem, (j, i, g), inside(i)
        )

    def target_copy(i):
        return remote(zstage.at[i], zgot.at[i], t_sem, (i,), inside(i))

    def back_copy(j, i, g):
        some = pl.ds(g * own_half, own_half)
        return remote(
            dqs.at[some, j * plane + i], ret.at[j, i, some], r_sem, (j, i, g), inside(i)
        )

    def back_copies(j, g):
        each(1, plane, lambda i: back_copy(j, i, g).start())

    def part_copy(j, h):
        return half_copy(pstage, part, p_sem, j, h, j, along(1 if j == 3 else j))

    for load in loads[0:3]:
        load.wait()
    for h in range(2):
        if h == 1:
            loads[3].wait()
        span = slice(h * piece, (h + 1) * piece)
        pre = jnp.dot(features[span, :], w_hidden[...], preferred_element_type=F32)
        gate = 1.0 / (1.0 + jnp.exp(-pre))
        active = (pre * gate).astype(BF16)
        hidden[span, :] = active
        slope[span, :] = pre
        qline[0, span, :] = jnp.dot(active, w_out[...], preferred_element_type=F32).astype(BF16)
        query_copy(2, h).start()
    for h in range(2):
        query_copy(1, h).start()

    for load in loads[4:6]:
        load.wait()
    for j in range(1, line):
        for copy in meta_copies(j):
            copy.start()
    earlier[...] = flags(iota((users, users), 0) < iota((users, users), 1))
    loads[6].wait()
    k = iota((hosted, 1), 0)
    host = lax.bitwise_xor(lax.shift_right_logical(k, log2(local_clusters)), p)
    slot = (z * plane + host) * local_clusters + (k & (local_clusters - 1))
    names = jnp.sum(
        jnp.where(slot_ref[...] == slot, iota((hosted, clusters), 1), 0).astype(F32),
        axis=1,
        keepdims=True,
    ).astype(I32)

    lane = iota((1, LANES), 1)
    zstage[...] = jnp.zeros(zstage.shape, F32)

    def choose(j):
        routes = routes_ref if j == 0 else metas.at[0, j]
        spots = spots_ref if j == 0 else metas.at[1, j]
        target = jnp.zeros((hosted, users), F32)
        for r in range(visits):
            same = names == routes[r : r + 1, :]
            target = jnp.where(same, (spots[r : r + 1, :] + 1).astype(F32), target)
        member = target > 0.0
        rank = jnp.dot(flags(member), earlier[...], preferred_element_type=F32)
        code = jnp.where(member, rank, -1.0)
        codes[...] = code
        found = zstage[...].reshape(hosted, LANES)
        for s in range(cap):
            spot = jnp.sum(jnp.where(code == float(s), target, 0.0), axis=1, keepdims=True)
            found = jnp.where(lane == j * cap + s, spot, found)
        zstage[...] = found.reshape(plane, local_clusters, LANES)

        def block(i):
            own = codes[pl.ds(pl.multiple_of(i * local_clusters, TILE), local_clusters), :]
            if cap % TILE == 0:
                seat = iota((1, cap, 1), 1).astype(F32)
                chosen = flags((own[:, None, :] == seat).reshape(rows, users))
            else:
                first = iota((rows, local_clusters), 1) * cap
                row = iota((rows, local_clusters), 0)
                spread = flags((row >= first) & (row < first + cap))
                seat = (iota((rows, 1), 0) & (cap - 1)).astype(F32)
                wide = jnp.dot(spread, own.astype(BF16), preferred_element_type=F32)
                chosen = flags(wide == seat)
            sel[j, i] = chosen

        each(0, plane, block)

    def seated(j, i):
        value = jnp.dot(sel[j, i], qline[j], preferred_element_type=F32)
        return value.reshape(local_clusters, cap, width).astype(BF16)

    def send_seats(j):
        def block(i):
            stage[j, i] = seated(j, i)
            seat_copy(j, i, 0).start()
            if j < line - 1:
                seat_copy(j, i, 1).start()

        each(1, plane, block)
        if j == line - 1:
            each(1, plane, lambda i: seat_copy(j, i, 1).start())
        got[:, j * plane] = seated(j, 0)

    def relay():
        for h in range(2):
            query_copy(2, h).wait_recv()
            query_copy(3, h).start()

    choose(0)
    send_seats(0)
    for j in range(1, line):
        for copy in meta_copies(j):
            copy.wait_recv()
        choose(j)
        if j == 2:
            relay()
    each(1, plane, lambda i: target_copy(i).start())
    zgot[0] = zstage[0]
    for h in range(2):
        query_copy(1, h).wait_recv()
    send_seats(1)
    send_seats(2)

    for load in loads[7:]:
        load.wait()
    for t in range(groups):
        here = slice(t * LANES, (t + 1) * LANES)
        count = counts[:, here]
        high = lax.shift_right_logical(count, 6)
        lookup[:, t, :] = ids[:, here].astype(F32)
        lookup[:, groups + t, :] = high.astype(F32)
        lookup[:, 2 * groups + t, :] = (count & 63).astype(F32)

    digit = 16
    tall = item_rows // digit
    chunk = mass_left.shape[1]
    mass_grid[...] = jnp.zeros(mass_grid.shape, F32)

    def weigh(t):
        here = pl.ds(pl.multiple_of(t * chunk, LANES), chunk)
        rest = 1.0 / counts[:, here].astype(F32)
        terms = []
        for _ in range(3):
            term = rest.astype(BF16).astype(F32)
            rest = rest - term
            terms.append(term)
        high = lax.shift_right_logical(ids[:, here], log2(digit))
        low = ids[:, here] & (digit - 1)
        for c in range(local_clusters):
            match = high[c : c + 1, :] == iota((tall, chunk), 0)
            mass_left[c * 3 * tall : (c + 1) * 3 * tall, :] = jnp.concatenate(
                [jnp.where(match, term[c : c + 1, :], 0.0) for term in terms], axis=0
            ).astype(BF16)
            mass_right[c * digit : (c + 1) * digit, :] = flags(
                low[c : c + 1, :] == iota((digit, chunk), 0)
            )
        mass_grid[...] += lax.dot_general(
            mass_left[...],
            mass_right[...],
            (((1,), (1,)), ((), ())),
            preferred_element_type=F32,
        )

    def settle_masses():
        across = local_clusters * digit
        column = iota((tall, across), 1)
        grid = jnp.zeros((tall, across), F32)
        for c in range(local_clusters):
            rows_c = mass_grid[c * 3 * tall : (c + 1) * 3 * tall, :]
            block = rows_c[0:tall] + rows_c[tall : 2 * tall] + rows_c[2 * tall : 3 * tall]
            grid = jnp.where(lax.shift_right_logical(column, log2(digit)) == c, block, grid)
        item = iota((item_rows, tall), 0)
        rise = jnp.where(
            lax.shift_right_logical(item, log2(digit)) == iota((item_rows, tall), 1), 1.0, 0.0
        )
        exact = lax.Precision.HIGHEST
        wide = jnp.dot(rise, grid, preferred_element_type=F32, precision=exact)
        same = (iota((item_rows, across), 0) & (digit - 1)) == (
            iota((item_rows, across), 1) & (digit - 1)
        )
        pick = jnp.where(
            lax.shift_right_logical(iota((across, local_clusters), 0), log2(digit))
            == iota((across, local_clusters), 1),
            1.0,
            0.0,
        )
        logs = jnp.log(
            jnp.dot(
                jnp.where(same, wide, 0.0), pick, preferred_element_type=F32, precision=exact
            )
        )
        for c in range(local_clusters):
            mass[c] = logs[:, c : c + 1]

    chunks = samples // chunk
    each(0, chunks, weigh)
    for h in range(2):
        query_copy(3, h).wait_recv()
    send_seats(3)
    settle_masses()
    pre = slope[...]
    gate = 1.0 / (1.0 + jnp.exp(-pre))
    slope[...] = gate * (1.0 + pre * (1.0 - gate))

    features_t[...] = features[...].T
    each(1, plane, lambda i: target_copy(i).wait_recv())

    entry = iota((LANES, seats), 0)
    column = iota((LANES, seats), 1)
    source = lax.shift_right_logical(column, log2(cap))
    place = lax.shift_right_logical(source, log2(plane)) * cap + (column & (cap - 1))
    widen = flags(entry == place)
    from_row = lax.shift_right_logical(iota((hosted, seats), 0), log2(local_clusters))
    from_column = lax.shift_right_logical(iota((hosted, seats), 1), log2(cap)) & (plane - 1)
    matched = from_row == from_column
    fold = flags(
        iota((local_clusters, hosted), 0)
        == (iota((local_clusters, hosted), 1) & (local_clusters - 1))
    )
    z_all = zgot[...].reshape(hosted, LANES)
    z_high = jnp.floor(z_all * (1.0 / 64.0))
    z_low = z_all - z_high * 64.0

    def regroup(value):
        spread = jnp.dot(value.astype(BF16), widen, preferred_element_type=F32)
        spread = jnp.where(matched, spread, 0.0).astype(BF16)
        return jnp.dot(fold, spread, preferred_element_type=F32)

    spots_all = (regroup(z_high) * 64.0 + regroup(z_low)).astype(I32)
    for c in range(local_clusters):
        tpos[c] = spots_all[c : c + 1, :]

    item_wide = iota((item_rows, seats), 0)
    low_wide = iota((LANES, seats), 0)
    high_wide = iota((groups, seats), 0)
    loss_lane = iota((1, loss_out.shape[1]), 1)
    together = 4

    def look_up(c):
        spot = tpos[c] - 1
        live = spot >= 0
        near = jnp.dot(
            lookup[c].astype(BF16),
            flags((spot & (LANES - 1)) == low_wide),
            preferred_element_type=F32,
        )
        here = lax.shift_right_logical(spot, log2(LANES)) == high_wide
        found = [
            jnp.sum(
                jnp.where(here, near[n * groups : (n + 1) * groups, :], 0.0), axis=0, keepdims=True
            )
            for n in range(3)
        ]
        own_item[c] = jnp.where(live, found[0], -1.0).astype(I32)
        own_count[c] = jnp.log(jnp.where(live, found[1] * 64.0 + found[2], 1.0))

    def look_up_some(n):
        for u in range(together):
            look_up(n * together + u)

    each(0, local_clusters // together, look_up_some)

    for j in range(line):
        for g in range(1 if j == line - 1 else 2):
            each(1, plane, lambda i: seat_copy(j, i, g).wait_recv())

    def own(c, losses):
        query = got[c].reshape(seats, width)
        block = items[c]
        scores = lax.dot_general(
            block, query, (((1,), (1,)), ((), ())), preferred_element_type=F32
        )
        shifted = scores + mass[c]
        top = jnp.max(shifted, axis=0, keepdims=True)
        expo = jnp.exp(shifted - top)
        total = jnp.sum(expo, axis=0, keepdims=True)
        mine = own_item[c]
        live = jnp.where(mine >= 0, 1.0, 0.0)
        hit = mine == item_wide
        picked = jnp.sum(jnp.where(hit, scores, 0.0), axis=0, keepdims=True) - own_count[c]
        loss = (jnp.log(total) + top - picked) * live
        mean = jnp.sum(loss, axis=1, keepdims=True) / jnp.sum(live, axis=1, keepdims=True)
        weight = (expo * (1.0 / total) - jnp.where(hit, 1.0, 0.0)).astype(BF16)
        wts[c] = weight
        dq = lax.dot_general(weight, block, (((0,), (0,)), ((), ())), preferred_element_type=F32)
        dqs[c] = dq.reshape(line * plane, cap, width).astype(BF16)
        return jnp.where(loss_lane == c, mean, losses)

    def own_some(n, losses):
        for u in range(together):
            losses = own(n * together + u, losses)
        return losses

    losses = lax.fori_loop(0, own_half // together, own_some, jnp.zeros(loss_out.shape, F32))
    for j in (3, 2):
        back_copies(j, 0)
    each(1, plane, lambda i: seat_copy(line - 1, i, 1).wait_recv())
    loss_out[...] = lax.fori_loop(
        own_half // together, local_clusters // together, own_some, losses
    )
    for j in (3, 2):
        back_copies(j, 1)
    for j in (1, 0):
        for g in range(2):
            back_copies(j, g)

    for j in range(line - 1, -1, -1):
        ret[j, 0] = dqs[:, j * plane]

    def tables(c):
        table_out[c] = jnp.dot(
            wts[c], got[c].reshape(seats, width), preferred_element_type=F32
        )

    each(0, local_clusters, tables)

    for j in range(1, line):
        for copy in meta_copies(j):
            copy.wait_send()
        for h in range(2):
            query_copy(j, h).wait_send()

    def forward_sent(i):
        target_copy(i).wait_send()
        for j in range(line):
            for g in range(2):
                seat_copy(j, i, g).wait_send()

    each(1, plane, forward_sent)

    def gather(j):
        for g in range(2):
            each(1, plane, lambda i: back_copy(j, i, g).wait_recv())
        return lax.dot_general(
            sel[j].reshape(plane * rows, users),
            ret[j].reshape(plane * rows, width),
            (((0,), (0,)), ((), ())),
            preferred_element_type=F32,
        )

    def push(j, value):
        pstage[j] = value.astype(BF16)
        for h in range(2):
            part_copy(j, h).start()

    push(3, gather(3))
    second = gather(2)
    for h in range(2):
        span = slice(h * piece, (h + 1) * piece)
        part_copy(3, h).wait_recv()
        pstage[2, span, :] = (second[span, :] + part[3, span, :].astype(F32)).astype(BF16)
        part_copy(2, h).start()
    push(1, gather(1))
    total = gather(0)
    for j in (1, 2):
        for h in range(2):
            part_copy(j, h).wait_recv()
        total = total + part[j].astype(F32)
    dq_total = total.astype(BF16)

    feat, hid = features.shape[1], hidden.shape[1]
    dhidden = lax.dot_general(
        dq_total, w_out[...], (((1,), (1,)), ((), ())), preferred_element_type=F32
    )
    dpre = (dhidden * slope[...]).astype(BF16)
    wide = 2 * LANES
    for b in range(hid // wide):
        product = jnp.dot(
            features_t[...], dpre[:, b * wide : (b + 1) * wide], preferred_element_type=F32
        )
        for h in range(2):
            acc[(2 * b + h) * feat : (2 * b + h + 1) * feat, :] = product[
                :, h * LANES : (h + 1) * LANES
            ]
    big_rows = feat * (hid // LANES)
    acc[big_rows : big_rows + hid, :] = lax.dot_general(
        hidden[...], dq_total, (((0,), (0,)), ((), ())), preferred_element_type=F32
    )
    if acc.shape[0] > big_rows + hid:
        spare = acc.shape[0] - big_rows - hid
        acc[big_rows + hid :, :] = jnp.zeros((spare, LANES), F32)

    chips = plane // 2
    core, chip = p % 2, p // 2
    cuts, half = summed_groups(line, chips, (feat + width) * hid)
    base = core * half
    away = (1 - core) * half

    def at(start, size):
        return pl.ds(pl.multiple_of(start, TILE), size)

    class Cut:
        def __init__(self, n):
            self.n = n
            self.plane_first, self.start, self.size = cuts[n]
            self.count1, self.count2 = (chips, line) if self.plane_first else (line, chips)
            self.size1 = self.size // self.count1
            self.size2 = self.size1 // self.count2
            self.in1, self.in2 = inboxes[2 * n], inboxes[2 * n + 1]

        def device1(self, i):
            return inside(2 * i) if self.plane_first else along(i)

        def device2(self, i):
            return along(i) if self.plane_first else inside(2 * i)

        def block(self, i):
            mine = chip if self.plane_first else z
            return base + self.start + flip(mine, i, self.count1) * self.size1

        def piece(self, i, j):
            mine = z if self.plane_first else chip
            return self.block(i) + flip(mine, j, self.count2) * self.size2

    cut = [Cut(n) for n in range(len(cuts))]
    started = []

    def give(start, size, inbox, sems, index, device):
        span = at(start, size)
        outb[span, :] = acc[span, :].astype(BF16)
        copy = remote(outb.at[span, :], inbox, sems, index, device)
        copy.start()
        started.append(copy)
        return copy

    def added(start, size, arrived):
        total = acc[at(start, size), :]
        for inbox in arrived:
            total = total + inbox.astype(F32)
        return total

    def share(start, size, sems, index, device):
        span = at(start, size)
        copy = remote(full.at[span, :], full.at[span, :], sems, index, device)
        copy.start()
        started.append(copy)
        return copy

    def finish(copies):
        for copy in copies:
            copy.wait_recv()

    first = [
        give(away + c.start, c.size, core_in.at[c.start : c.start + c.size, :], c_sem, (c.n,), inside(1))
        for c in cut
    ]

    def backward_sent(i):
        for j in range(line):
            for g in range(2):
                back_copy(j, i, g).wait_send()

    each(1, plane, backward_sent)
    for j in range(1, line):
        for h in range(2):
            part_copy(j, h).wait_send()

    second = []
    for c in cut:
        first[c.n].wait_recv()
        mine = base + c.start
        acc[at(mine, c.size), :] = added(mine, c.size, [core_in[c.start : c.start + c.size, :]])
        second.append(
            [
                give(c.block(i), c.size1, c.in1.at[i], s1_sem, (c.n, i), c.device1(i))
                for i in range(1, c.count1)
            ]
        )
    third = []
    for c in cut:
        finish(second[c.n])
        acc[at(c.block(0), c.size1), :] = added(
            c.block(0), c.size1, [c.in1[i] for i in range(1, c.count1)]
        )
        third.append(
            [
                give(c.piece(0, j), c.size2, c.in2.at[j], s2_sem, (c.n, j), c.device2(j))
                for j in range(1, c.count2)
            ]
        )
    outer, inner, last = {}, {}, []
    for c in cut:
        finish(third[c.n])
        mine = c.piece(0, 0)
        full[at(mine, c.size2), :] = added(
            mine, c.size2, [c.in2[j] for j in range(1, c.count2)]
        ).astype(BF16)
        for j in range(1, c.count2):
            inner[c.n, j] = share(mine, c.size2, g2_sem, (c.n, j), c.device2(j))
        for i in range(1, c.count1):
            outer[c.n, i, 0] = share(mine, c.size2, g1_sem, (c.n, i, 0), c.device1(i))
    for c in cut:
        for j in range(1, c.count2):
            inner[c.n, j].wait_recv()
            for i in range(1, c.count1):
                outer[c.n, i, j] = share(
                    c.piece(0, j), c.size2, g1_sem, (c.n, i, j), c.device1(i)
                )
        last.append(share(c.block(0), c.size1, go_sem, (c.n, 0), inside(1)))
    for c in cut:
        for i in range(1, c.count1):
            finish(outer[c.n, i, j] for j in range(c.count2))
            last.append(share(c.block(i), c.size1, go_sem, (c.n, i), inside(1)))
    finish(last)
    for b in range(hid // LANES):
        big_out[:, b * LANES : (b + 1) * LANES] = full[b * feat : (b + 1) * feat, :].astype(
            big_out.dtype
        )
    small_out[...] = full[big_rows : big_rows + hid, :].astype(small_out.dtype)

    for copy in started:
        copy.wait_send()


def local(
    features, w_hidden, w_out, items, routes, cluster_slot, sample_ids, sample_counts, positives
):
    devices = lax.axis_size("dev")
    line, plane = LINE, devices // LINE
    chips = plane // 2
    users, visits = routes.shape
    feat, hid = w_hidden.shape
    width = w_out.shape[1]
    clusters = cluster_slot.shape[0]
    local_clusters, samples = sample_ids.shape
    item_rows = items.shape[0] // local_clusters
    cap = max(2, 2 * users * visits // (local_clusters * devices))
    rows = local_clusters * cap
    hosted = plane * local_clusters
    seats = devices * cap
    groups = samples // LANES
    cuts, half = summed_groups(line, chips, (feat + width) * hid)
    most = max(chips, line)
    inboxes = []
    for plane_first, _, size in cuts:
        count1, count2 = (chips, line) if plane_first else (line, chips)
        inboxes.append(pltpu.VMEM((count1, size // count1, LANES), BF16))
        inboxes.append(pltpu.VMEM((count2, size // count1 // count2, LANES), BF16))
    vmem = pl.BlockSpec(memory_space=pltpu.VMEM)
    hbm = pl.BlockSpec(memory_space=pltpu.HBM)
    dma = pltpu.SemaphoreType.DMA
    loss, big, small, table = pl.pallas_call(
        functools.partial(step_kernel, line, plane, cap),
        out_shape=(
            jax.ShapeDtypeStruct((1, local_clusters), F32),
            jax.ShapeDtypeStruct((feat, hid), OUT),
            jax.ShapeDtypeStruct((hid, width), OUT),
            jax.ShapeDtypeStruct((local_clusters, item_rows, width), F32),
        ),
        in_specs=[hbm] * 9,
        out_specs=[vmem] * 4,
        scratch_shapes=[
            pltpu.VMEM((users, feat), BF16),
            pltpu.VMEM((feat, users), BF16),
            pltpu.VMEM((feat, hid), BF16),
            pltpu.VMEM((hid, width), BF16),
            pltpu.VMEM((local_clusters, item_rows, width), BF16),
            pltpu.VMEM((local_clusters, samples), I32),
            pltpu.VMEM((local_clusters, samples), I32),
            pltpu.VMEM((visits, users), I32),
            pltpu.VMEM((visits, users), I32),
            pltpu.VMEM((1, clusters), I32),
            pltpu.VMEM((users, hid), F32),
            pltpu.VMEM((users, hid), BF16),
            pltpu.VMEM((2, line, visits, users), I32),
            pltpu.VMEM((line, users, width), BF16),
            pltpu.VMEM((users, users), BF16),
            pltpu.VMEM((hosted, users), F32),
            pltpu.VMEM((line, plane, rows, users), BF16),
            pltpu.VMEM((line, plane, local_clusters, cap, width), BF16),
            pltpu.VMEM((local_clusters, devices, cap, width), BF16),
            pltpu.VMEM((plane, local_clusters, LANES), F32),
            pltpu.VMEM((plane, local_clusters, LANES), F32),
            pltpu.VMEM((local_clusters, 3 * groups, LANES), F32),
            pltpu.VMEM((3 * local_clusters * (item_rows // 16), min(1024, samples)), BF16),
            pltpu.VMEM((16 * local_clusters, min(1024, samples)), BF16),
            pltpu.VMEM((3 * local_clusters * (item_rows // 16), 16 * local_clusters), F32),
            pltpu.VMEM((local_clusters, item_rows, 1), F32),
            pltpu.VMEM((local_clusters, 1, seats), I32),
            pltpu.VMEM((local_clusters, 1, seats), I32),
            pltpu.VMEM((local_clusters, 1, seats), F32),
            pltpu.VMEM((local_clusters, item_rows, seats), BF16),
            pltpu.VMEM((local_clusters, devices, cap, width), BF16),
            pltpu.VMEM((line, plane, local_clusters, cap, width), BF16),
            pltpu.VMEM((line, users, width), BF16),
            pltpu.VMEM((line, users, width), BF16),
            pltpu.VMEM((2 * half, LANES), F32),
            pltpu.VMEM((2 * half, LANES), BF16),
            pltpu.VMEM((half, LANES), BF16),
            inboxes,
            pltpu.VMEM((2 * half, LANES), BF16),
            dma((10,)),
            dma((2, 2, line)),
            dma((2, line, 2)),
            dma((2, line, plane, 2)),
            dma((2, plane)),
            dma((2, line, plane, 2)),
            dma((2, line, 2)),
            dma((2, len(cuts))),
            dma((2, len(cuts), most)),
            dma((2, len(cuts), most)),
            dma((2, len(cuts), most, most)),
            dma((2, len(cuts), most)),
            dma((2, len(cuts), most)),
        ],
        compiler_params=pltpu.CompilerParams(
            collective_id=0, has_side_effects=True, vmem_limit_bytes=VMEM_BYTES
        ),
        name="step",
    )(
        *(
            pltpu.with_memory_space_constraint(array, pltpu.HBM)
            for array in (
                features,
                w_hidden,
                w_out,
                items.reshape(local_clusters, item_rows, width),
                sample_ids,
                sample_counts,
                routes.T,
                positives.T,
                cluster_slot.reshape(1, clusters),
            )
        )
    )
    return finish(loss, big, small, table.reshape(items.shape))


def finish_kernel(loss_ref, big_ref, small_ref, table_ref, loss_out, big_out, small_out, table_out):
    loss_out[...] = loss_ref[...].reshape(loss_out.shape)
    big_out[...] = big_ref[...].astype(F32)
    small_out[...] = small_ref[...].astype(F32)
    table_out[...] = table_ref[...]


def finish(loss, big, small, table):
    steps = 2

    def cut(array):
        shape = array.shape
        return pl.BlockSpec((shape[0] // steps, shape[1]), lambda n: (n, 0))

    specs = [cut(big), cut(small), cut(table)]
    return pl.pallas_call(
        finish_kernel,
        grid=(steps,),
        out_shape=(
            jax.ShapeDtypeStruct(loss.shape[1:], F32),
            jax.ShapeDtypeStruct(big.shape, F32),
            jax.ShapeDtypeStruct(small.shape, F32),
            jax.ShapeDtypeStruct(table.shape, F32),
        ),
        in_specs=[pl.BlockSpec(loss.shape, lambda n: (0, 0))] + specs,
        out_specs=[pl.BlockSpec(loss.shape[1:], lambda n: (0,))] + specs,
        compiler_params=pltpu.CompilerParams(vmem_limit_bytes=VMEM_BYTES),
        name="finish",
    )(loss, big, small, table)


OUT = BF16


def solution(mesh):
    in_specs = (
        P("dev", None),
        P(),
        P(),
        P("dev", None),
        P("dev", None),
        P(),
        P("dev", None),
        P("dev", None),
        P("dev", None),
    )
    out_specs = (P("dev"), P(), P(), P("dev", None))
    return jax.shard_map(local, mesh=mesh, in_specs=in_specs, out_specs=out_specs, check_vma=False)
```
